512 devices in a mesh: tm: 16 (over z_lo, core), space: 32 (over y, x, z_hi).
Axes of the slice: x: 4, y: 4, z: 16 (z_hi: 2, z_lo: 8; z = z_hi * 8 + z_lo), core: 2. Of those that a mesh axis runs over, the one named last changes fastest.
Arguments:
- vectors: bfloat16 [16, 2, 32, 3, 256, 128], P('tm', None, 'space'), may hold values from -12 to 12
- gauge_links: float32 [16, 3, 2, 32, 3, 3, 128], P('tm', None, None, 'space'), may hold values from -2.5 to 2.5
- perambulator: bfloat16 [16, 256, 2, 256, 256], P('tm', 'space'), may hold values from -0.375 to 0.375
- directions: int32 [16], P('tm'), may hold values from 0 to 2
- momentum: int32 [3], replicated, may hold values from -2 to 2
- source_list: int32 [16], replicated, may hold values from 0 to 15, each once
Outputs:
- elementals: bfloat16 [16, 256, 2, 256], P('tm', 'space')
- correlator: float32 [2, 16, 16], P(None, 'tm')
The draws below stay inside these ranges and needn't reach their ends.
Inputs may be any that keep to these rules, and one draw needn't show every extreme that they name: `directions`: 0, 1, 2 stand for x, y, z. `source_list`: each timeslice is the source of exactly one slot.
All inputs are finite; a program needn't handle non-finite values.
Results may differ from the reference program's by a relative error of at most 0.019.
Values may be sent and summed in bfloat16 or wider, within the bound.
No kernel may reach another device: no remote copies, remote signals or barrier semaphores. Data moves between devices by JAX's collectives and lax.ppermute only.
A program may use at most 64 MiB of HBM per device.

```python
import math
import jax
import jax.numpy as jnp
from jax import lax

NV = 256
NS = 4
SX = 16
SY = 8
SMEAR = 2
NT = 16
LZ = 32


def set_ends(values, rng, low, largest):
    index_at = [jax.random.randint(jax.random.fold_in(rng, axis), (), 0, length) for axis, length in enumerate(values.shape)]
    widest = values.shape.index(max(values.shape))
    next_to = index_at[:widest] + [(index_at[widest] + 1) % values.shape[widest]] + index_at[widest + 1:]
    return values.at[tuple(index_at)].set(low).at[tuple(next_to)].set(largest)


def block_scale(stream_key, dims, cuts, smallest, top_value):
    loudness, own = 1.0, jax.random.fold_in(stream_key, 6)
    for dim, shards_of in cuts:
        draws = jnp.exp(jax.random.uniform(jax.random.fold_in(own, dim), (shards_of,), jnp.float32, smallest / len(cuts), top_value / len(cuts)))
        loudness = loudness * jnp.repeat(draws, dims[dim] // shards_of).reshape([-1 if axis == dim else 1 for axis in range(len(dims))])
    return loudness


def scatter_about(rng, dims, deviation, most, pieces=(), kind=jnp.bfloat16):
    entries = deviation * jax.random.normal(rng, dims, jnp.float32)
    if pieces:
        entries = entries * block_scale(rng, dims, pieces, -0.22, 0.18)
    return jnp.clip(entries, -most, most).astype(kind)


def setup_inputs(seed: int = 0) -> dict:
    key_list = jax.random.split(jax.random.key(seed), 7)
    vectors = scatter_about(key_list[0], (NT, 2, LZ, 3, NV, SX * SY), 2.0, 12.0, ((0, 16), (2, 32)))
    gauge_links = scatter_about(key_list[1], (NT, 3, 2, LZ, 3, 3, SX * SY), 0.4, 2.5, ((0, 16), (3, 32)), jnp.float32)
    perambulator = scatter_about(key_list[2], (NT, NT * NS * NS, 2, NV, NV), NV ** -0.5, 0.375, ((0, 16), (1, 32)))
    directions = set_ends(jax.random.randint(key_list[3], (NT,), 0, 3), jax.random.fold_in(key_list[3], 1), 0, 2).astype(jnp.int32)
    momentum = jax.random.randint(key_list[4], (3,), -2, 3).astype(jnp.int32)
    source_list = jax.random.permutation(key_list[5], NT).astype(jnp.int32)
    return dict(vectors=vectors, gauge_links=gauge_links, perambulator=perambulator, directions=directions, momentum=momentum, source_list=source_list)


smear_kappa = 0.05

def colour_apply(link_field, colour_field, adjoint):
    if adjoint:
        link_real = jnp.swapaxes(link_field[0], 1, 2)
        link_imag = -jnp.swapaxes(link_field[1], 1, 2)
    else:
        link_real = link_field[0]
        link_imag = link_field[1]

    def contract(matrix, vector):
        return lax.optimization_barrier(jnp.sum(matrix[:, :, :, None, :] * vector[:, None, :, :, :], axis=2))
    out_real = contract(link_real, colour_field[0]) - contract(link_imag, colour_field[1])
    out_imag = contract(link_real, colour_field[1]) + contract(link_imag, colour_field[0])
    return jnp.stack([out_real, out_imag])

def ahead_x(colour_field):
    column = jnp.arange(colour_field.shape[-1]) % SX
    return jnp.where(column == SX - 1, jnp.roll(colour_field, SX - 1, axis=-1), jnp.roll(colour_field, -1, axis=-1))

def behind_x(colour_field):
    column = jnp.arange(colour_field.shape[-1]) % SX
    return jnp.where(column == 0, jnp.roll(colour_field, 1 - SX, axis=-1), jnp.roll(colour_field, 1, axis=-1))

def rounded_copy(colour_field):
    return lax.optimization_barrier(colour_field.astype(jnp.bfloat16)).astype(jnp.float32)

def smear_once(smeared, link_set):
    colour_field = smeared.astype(jnp.float32)
    summed = -6.0 * colour_field
    for direction in range(3):
        link_field = link_set[direction]
        if direction == 0:
            incoming = ahead_x(colour_field)
        elif direction == 1:
            incoming = jnp.roll(colour_field, -SX, axis=-1)
        else:
            incoming = jnp.roll(colour_field, -1, axis=1)
        carried = colour_apply(link_field, colour_field, True)
        if direction == 0:
            outgoing = behind_x(carried)
        elif direction == 1:
            outgoing = jnp.roll(carried, SX, axis=-1)
        else:
            outgoing = jnp.roll(rounded_copy(carried), 1, axis=1)
        summed = summed + colour_apply(link_field, incoming, False) + outgoing
    return (colour_field + smear_kappa * summed).astype(jnp.bfloat16)

def covariant_step(smeared, link_set, pick):
    colour_field = smeared.astype(jnp.float32)
    link_field = lax.dynamic_index_in_dim(link_set, pick, 0, keepdims=False)
    incoming = jnp.where(pick == 0, ahead_x(colour_field), jnp.where(pick == 1, jnp.roll(colour_field, -SX, axis=-1), jnp.roll(colour_field, -1, axis=1)))
    carried = colour_apply(link_field, colour_field, True)
    outgoing = jnp.where(pick == 0, behind_x(carried), jnp.where(pick == 1, jnp.roll(carried, SX, axis=-1), jnp.roll(rounded_copy(carried), 1, axis=1)))
    return colour_apply(link_field, incoming, False) - outgoing

def phase_angle(momentum, plane_index, extent):
    site_index = jnp.arange(SX * SY)
    column = (site_index % SX).astype(jnp.float32)
    row_index = (site_index // SX).astype(jnp.float32)
    moment = momentum.astype(jnp.float32)
    return 2.0 * math.pi * (moment[0] * column[None, :] / SX + moment[1] * row_index[None, :] / SY + moment[2] * plane_index.astype(jnp.float32)[:, None] / extent)

def project_pair(gradient, angle_grid):
    cosine = jnp.cos(angle_grid)[:, None, None, :]
    sine_part = jnp.sin(angle_grid)[:, None, None, :]
    projected = jnp.stack([cosine * gradient[0] + sine_part * gradient[1], cosine * gradient[1] - sine_part * gradient[0]]).astype(jnp.bfloat16)
    return jnp.stack([projected, jnp.stack([projected[1], -projected[0]])])

def pair_trace(sink, partner, block_set):
    highest = lax.Precision.HIGHEST
    left_side = jnp.stack([jnp.stack([sink[:, 0], -sink[:, 1]], 1), jnp.stack([sink[:, 1], sink[:, 0]], 1)])
    right_side = jnp.stack([jnp.stack([partner[:, 0], partner[:, 1]]), jnp.stack([-partner[:, 1], partner[:, 0]])])
    block_float = block_set.astype(jnp.float32)
    first = jnp.einsum('pirk,brkj->pbij', left_side.astype(jnp.float32), block_float, precision=highest)
    first = rounded_copy(first)
    second = jnp.einsum('pbik,pqkj->qbij', first, right_side.astype(jnp.float32), precision=highest)
    trace_real = jnp.sum(second[0] * block_float[:, 0] + second[1] * block_float[:, 1])
    trace_imag = jnp.sum(second[1] * block_float[:, 0] - second[0] * block_float[:, 1])
    return jnp.stack([trace_real, trace_imag]) / (NS * NV)

def reference(vectors, gauge_links, perambulator, directions, momentum, source_list):
    angle_grid = phase_angle(momentum, jnp.arange(LZ), LZ)
    scale_factor = 1.0 / math.sqrt(3 * SX * SY * LZ)

    def one_slice(inputs):
        smeared, link_set, pick = inputs
        for sweep_index in range(SMEAR):
            smeared = smear_once(smeared, link_set)
        gradient = covariant_step(smeared, link_set, pick)
        paired = project_pair(gradient, angle_grid)
        partial_value = jnp.einsum('rzcas,orzcbs->aob', smeared.astype(jnp.float32), paired.astype(jnp.float32), precision=lax.Precision.HIGHEST)
        return (partial_value * scale_factor).astype(jnp.bfloat16)
    elementals = lax.map(one_slice, (vectors, gauge_links, directions))
    blocks_all = perambulator.reshape(NT, NT, NS * NS, 2, NV, NV)

    def one_sink(inputs):
        sink, sink_blocks = inputs

        def one_pair(pair_inputs):
            block_set, source = pair_inputs
            partner = lax.dynamic_index_in_dim(elementals, source, 0, keepdims=False)
            return pair_trace(sink, partner, block_set)
        return lax.map(one_pair, (sink_blocks, source_list))
    slot_values = lax.map(one_sink, (elementals, blocks_all))
    one_hot = (source_list[:, None] == jnp.arange(NT)[None, :]).astype(jnp.float32)
    correlator = jnp.einsum('tko,ks->ots', slot_values, one_hot, precision=lax.Precision.HIGHEST)
    return (elementals, correlator)
```

```python
import functools
import math

import jax
import jax.numpy as jnp
from jax import lax
from jax.experimental import pallas as pl
from jax.experimental.pallas import tpu as pltpu
from jax.sharding import Mesh, PartitionSpec as P

NV = 256
NS = 4
SX = 16
SY = 8
SITES = SX * SY
HALF = NV // 2
VROWS = 6 * HALF
LROWS = 64
KAPPA = 0.05

SPACE = ("y", "x", "zh")
XY = ("y", "x")
COLUMN = ("zl", "core", "zh")
CHUNK = 16


def whole():
    return pl.BlockSpec(memory_space=pltpu.VMEM)


def scalar():
    return pl.BlockSpec(memory_space=pltpu.SMEM)


def roll_lanes(value, shift):
    return pltpu.roll(value, shift % SITES, value.ndim - 1)


def ahead_x(value, last):
    return jnp.where(last, roll_lanes(value, SX - 1), roll_lanes(value, -1))


def behind_x(value, first):
    return jnp.where(first, roll_lanes(value, 1 - SX), roll_lanes(value, 1))


def smear_kernel(pick_ref, phase_ref, low_ref, mid_ref, high_ref, far_ref, left_ref, right_ref, link_ref, one_ref, two_ref):
    lane = lax.broadcasted_iota(jnp.int32, (18, SITES), 1) % SX
    for plane in range(6):
        source = (low_ref, mid_ref, high_ref)[plane // 2]
        block = source[plane % 2, pl.ds(VROWS, LROWS), :].astype(jnp.float32)
        link_ref[plane, pl.ds(0, LROWS), :] = block
        link_ref[plane, pl.ds(64, 18), :] = behind_x(block[0:18], lane == 0)
        link_ref[plane, pl.ds(88, 18), :] = roll_lanes(block[18:36], SX)

    def link(plane, base):
        return lambda part, row, column: link_ref[plane, pl.ds(base + part * 9 + row * 3 + column, 1), :]

    def apply(total, matrix, field, adjoint):
        for row in range(3):
            for column in range(3):
                if adjoint:
                    real, imag = matrix(0, column, row), matrix(1, column, row)
                    total[0][row] += real * field[0][column] + imag * field[1][column]
                    total[1][row] += real * field[1][column] - imag * field[0][column]
                else:
                    real, imag = matrix(0, row, column), matrix(1, row, column)
                    total[0][row] += real * field[0][column] - imag * field[1][column]
                    total[1][row] += real * field[1][column] + imag * field[0][column]

    column_of = lax.broadcasted_iota(jnp.int32, (CHUNK, SITES), 1) % SX
    last, first = column_of == SX - 1, column_of == 0
    pick = pick_ref[0]

    def each(field, change):
        return [[change(field[part][colour]) for colour in range(3)] for part in range(2)]

    def zeros():
        zero = jnp.zeros((CHUNK, SITES), jnp.float32)
        return [[zero for _ in range(3)] for _ in range(2)]

    def sweep(plane, here, above, below):
        total = zeros()
        apply(total, link(plane, 0), each(here, lambda v: ahead_x(v, last)), False)
        apply(total, link(plane, 64), each(here, lambda v: behind_x(v, first)), True)
        apply(total, link(plane, 18), each(here, lambda v: roll_lanes(v, -SX)), False)
        apply(total, link(plane, 88), each(here, lambda v: roll_lanes(v, SX)), True)
        apply(total, link(plane, 36), above, False)
        apply(total, link(plane - 1, 36), below, True)
        return [
            [
                here[part][colour] + KAPPA * (total[part][colour] - 6.0 * here[part][colour])
                for colour in range(3)
            ]
            for part in range(2)
        ]

    def rounded(value):
        return value.astype(jnp.bfloat16).astype(jnp.float32)

    def step(chunk, carry):
        start = pl.multiple_of(chunk * CHUNK, CHUNK)

        def start_field(plane):
            def get(part, colour):
                rows = pl.ds((part * 3 + colour) * HALF + start, CHUNK)
                if plane == 6:
                    return far_ref[rows, :].astype(jnp.float32)
                source = (low_ref, mid_ref, high_ref)[plane // 2]
                return source[plane % 2, rows, :].astype(jnp.float32)

            return [[get(part, colour) for colour in range(3)] for part in range(2)]

        def stored(ref, plane):
            return [[ref[plane, part * 3 + colour] for colour in range(3)] for part in range(2)]

        for plane in range(1, 6):
            result = sweep(plane, start_field(plane), start_field(plane + 1), start_field(plane - 1))
            for part in range(2):
                for colour in range(3):
                    one_ref[plane, part * 3 + colour] = rounded(result[part][colour])
        for plane in range(2, 5):
            result = sweep(plane, stored(one_ref, plane), stored(one_ref, plane + 1), stored(one_ref, plane - 1))
            for part in range(2):
                for colour in range(3):
                    two_ref[plane, part * 3 + colour] = rounded(result[part][colour])
        for side in range(2):
            plane = side + 2
            here, above = stored(two_ref, plane), stored(two_ref, plane + 1)
            incoming = [
                [
                    jnp.where(
                        pick == 0,
                        ahead_x(here[part][colour], last),
                        jnp.where(pick == 1, roll_lanes(here[part][colour], -SX), above[part][colour]),
                    )
                    for colour in range(3)
                ]
                for part in range(2)
            ]
            moved = zeros()
            apply(moved, link(plane, pick * 18), incoming, False)

            def row_of(index):
                return phase_ref[pl.ds(side * 4 + index, 1), :]

            for colour in range(3):

                def put(kind, part, left, real, imag):
                    index = ((kind * 2 + part) * 2 + side) * 3 + colour
                    lanes = pl.ds((index % 2) * SITES, SITES)
                    left_ref[index // 2, pl.ds(start, CHUNK), lanes] = left.astype(jnp.bfloat16)
                    right_ref[index // 2, pl.ds(start, CHUNK), lanes] = real.astype(jnp.bfloat16)
                    right_ref[index // 2, pl.ds(HALF + start, CHUNK), lanes] = imag.astype(jnp.bfloat16)

                def turned(field, base):
                    cosine, sine = row_of(base), row_of(base + 1)
                    return (
                        cosine * field[0][colour] - sine * field[1][colour],
                        cosine * field[1][colour] + sine * field[0][colour],
                    )

                real, imag = turned(moved, 0)
                put(0, 0, here[0][colour], real, imag)
                put(0, 1, here[1][colour], imag, -real)
                real, imag = turned(here, 2)
                put(1, 0, moved[0][colour], real, imag)
                put(1, 1, moved[1][colour], imag, -real)
        return carry

    lax.fori_loop(0, HALF // CHUNK, step, 0)


def smear(pick, phase, low, mid, high, far):
    return pl.pallas_call(
        smear_kernel,
        out_shape=(
            jax.ShapeDtypeStruct((12, HALF, 2 * SITES), jnp.bfloat16),
            jax.ShapeDtypeStruct((12, 2 * HALF, 2 * SITES), jnp.bfloat16),
        ),
        in_specs=[scalar(), whole(), whole(), whole(), whole(), whole()],
        out_specs=(whole(), whole()),
        scratch_shapes=[
            pltpu.VMEM((6, 112, SITES), jnp.float32),
            pltpu.VMEM((6, 6, CHUNK, SITES), jnp.float32),
            pltpu.VMEM((5, 6, CHUNK, SITES), jnp.float32),
        ],
        name="smear",
    )(pick, phase, low, mid, high, far)


def pair_kernel(core_ref, own_ref, other_ref, right_ref, out_ref):
    core = core_ref[0]

    def product(ref):
        total = jnp.zeros((HALF, 2 * HALF), jnp.float32)
        for index in range(12):
            total += lax.dot_general(
                ref[index], right_ref[index], (((1,), (1,)), ((), ())), preferred_element_type=jnp.float32
            )
        return total

    out_ref[pl.ds(pl.multiple_of(core * HALF, HALF), HALF), :] = product(own_ref)
    out_ref[pl.ds(pl.multiple_of((1 - core) * HALF, HALF), HALF), :] = product(other_ref)


def pair(core, own, other, right):
    return pl.pallas_call(
        pair_kernel,
        out_shape=jax.ShapeDtypeStruct((NV, 2 * HALF), jnp.float32),
        in_specs=[scalar(), whole(), whole(), whole()],
        out_specs=whole(),
        name="pair",
    )(core, own, other, right)


def spread_kernel(time_ref, source_ref, gathered_ref, out_ref):
    slots = out_ref.shape[0]

    def fetch(time):
        parts = [gathered_ref[(time // 2) * 4 + half * 2 + time % 2] for half in range(2)]
        return jnp.concatenate(
            [parts[half][:, part * HALF : (part + 1) * HALF] for part in range(2) for half in range(2)], axis=1
        )

    own = fetch(time_ref[0])
    for slot in range(slots):
        out_ref[slot, 0] = own
        out_ref[slot, 1] = fetch(source_ref[slot])


def spread(time, source_list, gathered):
    rows = gathered.shape[1]
    return pl.pallas_call(
        spread_kernel,
        out_shape=jax.ShapeDtypeStruct((source_list.shape[0], 2, rows, 2 * NV), jnp.bfloat16),
        in_specs=[scalar(), scalar(), whole()],
        out_specs=whole(),
        name="spread",
    )(time, source_list, gathered)


def trace_kernel(sink_ref, source_ref, block_ref, out_ref, left_ref):
    real, imag = sink_ref[:, :NV], sink_ref[:, NV:]
    left_ref[:NV, :NV] = real
    left_ref[:NV, NV:] = -imag
    left_ref[NV:, :NV] = imag
    left_ref[NV:, NV:] = real

    def folded(value):
        return jnp.sum(value.reshape(NV // 8, 8, NV), axis=0)

    def step(index, totals):
        block = block_ref[index]
        first = jnp.dot(left_ref[...], block, preferred_element_type=jnp.float32).astype(jnp.bfloat16)
        second = jnp.dot(first, source_ref[...], preferred_element_type=jnp.float32)
        second_real = second[:NV, :NV] - second[NV:, NV:]
        second_imag = second[:NV, NV:] + second[NV:, :NV]
        block_real = block[:NV].astype(jnp.float32)
        block_imag = block[NV:].astype(jnp.float32)
        return (
            totals[0] + folded(second_real * block_real + second_imag * block_imag),
            totals[1] + folded(second_imag * block_real - second_real * block_imag),
        )

    zero = jnp.zeros((8, NV), jnp.float32)
    totals = lax.fori_loop(0, block_ref.shape[0], step, (zero, zero))
    lane = lax.broadcasted_iota(jnp.int32, out_ref.shape, 1)
    out_ref[...] = jnp.where(lane == 0, jnp.sum(totals[0]), jnp.sum(totals[1]))


def trace(sink, source, blocks, copies):
    return pl.pallas_call(
        trace_kernel,
        out_shape=jax.ShapeDtypeStruct((copies, 128), jnp.float32),
        in_specs=[whole(), whole(), whole()],
        out_specs=whole(),
        scratch_shapes=[pltpu.VMEM((2 * NV, 2 * NV), jnp.bfloat16)],
        name="trace",
    )(sink, source, blocks)


def phases(momentum, pick, pair_index, extent):
    site = jnp.arange(SITES)
    column = (site % SX).astype(jnp.float32)
    row = (site // SX).astype(jnp.float32)
    moment = momentum.astype(jnp.float32)
    height = (pair_index * 2 + jnp.arange(2)).astype(jnp.float32)
    angle = (
        2.0
        * math.pi
        * (moment[0] * column[None] / SX + moment[1] * row[None] / SY + moment[2] * height[:, None] / extent)
    )
    step = jnp.where(pick == 0, moment[0] / SX, jnp.where(pick == 1, moment[1] / SY, moment[2] / extent))
    shifted = angle + 2.0 * math.pi * step
    return jnp.stack([jnp.cos(angle), -jnp.sin(angle), -jnp.cos(shifted), jnp.sin(shifted)], axis=1).reshape(8, SITES)


def per_device(vectors, gauge_links, perambulator, directions, momentum, source_list):
    core = lax.axis_index("core")
    level = lax.axis_index("zh")
    pair_index = lax.axis_index(XY)
    pairs = lax.axis_size(XY)
    rows = NV // pairs

    halves = vectors[0, :, 0].reshape(6, 2, HALF, SITES)
    link_rows = gauge_links[0, :, :, 0].reshape(54, SITES).astype(jnp.bfloat16)
    pick_row = jnp.broadcast_to(directions[0].astype(jnp.bfloat16), (LROWS - 54, SITES))
    tail = jnp.concatenate([link_rows, pick_row], axis=0)

    def half_of(index):
        half = lax.dynamic_index_in_dim(halves, index, 1, keepdims=False).reshape(VROWS, SITES)
        return jnp.concatenate([half, tail], axis=0)

    kept = half_of(level)
    given = half_of(1 - level)
    crossed = lax.ppermute(kept, ("core", "zh"), [(1, 2), (2, 1)])
    taken = lax.ppermute(given, ("core", "zh"), [(0, 2), (3, 1), (1, 0), (2, 3)])
    same = core == level
    own_plane = jnp.where(same, kept, taken)
    other_plane = jnp.where(same, taken, crossed)
    even = level == 0
    mid = jnp.stack([jnp.where(even, own_plane, other_plane), jnp.where(even, other_plane, own_plane)])

    def moved(value, distance):
        return lax.ppermute(value, XY, [(i, (i + distance) % pairs) for i in range(pairs)])

    high = moved(mid, -1)
    low = moved(mid, 1)
    far = moved(mid[0, :VROWS], -2)
    pick = mid[0, VROWS + 54, 0].astype(jnp.int32)
    phase = phases(momentum, pick, pair_index, 2 * pairs)
    left, right = smear(pick[None], phase, low, mid, high, far)
    other = lax.ppermute(left, "core", [(0, 1), (1, 0)])
    partial_value = pair(core[None], left, other, right)

    parts = lax.all_to_all(partial_value, XY, 0, 0, tiled=True).reshape(pairs, rows, 2 * HALF)
    scale = 1.0 / math.sqrt(3 * SITES * 2 * pairs)
    share = (jnp.sum(parts, axis=0) * scale).astype(jnp.bfloat16)

    column = lax.axis_size(COLUMN)
    copies = jnp.broadcast_to(share[None], (column, rows, 2 * HALF))
    gathered = lax.all_to_all(copies, COLUMN, 0, 0, tiled=True)
    time = lax.axis_index(("zl", "core"))
    sent = spread(time[None], source_list, gathered)
    arrived = lax.all_to_all(sent, XY, 0, 0, tiled=True)
    sink = arrived[:, 0].reshape(NV, 2 * NV)
    source = arrived[:, 1].reshape(NV, 2 * NV)

    space_count = lax.axis_size(SPACE)
    own_rows = NV // space_count
    elemental = lax.dynamic_slice_in_dim(sink, lax.axis_index(SPACE) * own_rows, own_rows, 0)
    blocks = perambulator[0].reshape(-1, 2 * NV, NV)
    value = trace(sink, source, blocks, space_count)
    values = lax.all_to_all(value, SPACE, 0, 0, tiled=True)[:, :2].reshape(pairs, 2, 2)
    per_slot = jnp.sum(values, axis=1) / (NS * NV)
    one_hot = (source_list[:, None] == jnp.arange(source_list.shape[0])[None]).astype(jnp.float32)
    correlator = jnp.sum(per_slot[:, :, None] * one_hot[:, None, :], axis=0)
    return elemental.reshape(1, own_rows, 2, NV), correlator[:, None, :]


def solution(mesh):
    grid = Mesh(mesh.devices.reshape(8, 2, 4, 4, 2), ("zl", "core", "y", "x", "zh"))
    times = ("zl", "core")
    in_specs = (
        P(times, None, SPACE, None, None, None),
        P(times, None, None, SPACE, None, None, None),
        P(times, SPACE, None, None, None),
        P(times),
        P(),
        P(),
    )
    out_specs = (P(times, SPACE, None, None), P(None, times, None))
    return jax.shard_map(per_device, mesh=grid, in_specs=in_specs, out_specs=out_specs, check_vma=False)
```

```python
import math

import jax
import jax.numpy as jnp
from jax import lax
from jax.experimental import pallas as pl
from jax.experimental.pallas import tpu as pltpu
from jax.sharding import Mesh, PartitionSpec as P

NV = 256
NS = 4
SX = 16
SY = 8
SITES = SX * SY
HALF = NV // 2
VROWS = 6 * HALF
LROWS = 64
KAPPA = 0.05

SPACE = ("y", "x", "zh")
XY = ("y", "x")
CHUNK = 16


def whole():
    return pl.BlockSpec(memory_space=pltpu.VMEM)


def scalar():
    return pl.BlockSpec(memory_space=pltpu.SMEM)


def roll_lanes(value, shift):
    return pltpu.roll(value, shift % SITES, value.ndim - 1)


def ahead_x(value, last):
    return jnp.where(last, roll_lanes(value, SX - 1), roll_lanes(value, -1))


def behind_x(value, first):
    return jnp.where(first, roll_lanes(value, 1 - SX), roll_lanes(value, 1))


def smear_kernel(pick_ref, phase_ref, low_ref, mid_ref, high_ref, far_ref, left_ref, right_ref, link_ref, one_ref, two_ref):
    site = lax.broadcasted_iota(jnp.int32, (18, SITES), 1) % SX
    for plane in range(6):
        source = (low_ref, mid_ref, high_ref)[plane // 2]
        block = source[plane % 2, pl.ds(VROWS, LROWS), :].astype(jnp.float32)
        rows = [block[index : index + 1] for index in range(54)]
        if plane:
            behind = behind_x(block[0:18], site == 0)
            below = roll_lanes(block[18:36], SX)
            rows += [behind[index : index + 1] for index in range(18)]
            rows += [below[index : index + 1] for index in range(18)]
        for index in range(36 if plane == 0 else 0, len(rows)):
            link_ref[plane, index] = jnp.broadcast_to(rows[index], (CHUNK, SITES)).astype(jnp.bfloat16)

    def link(plane, base):
        return lambda part, row, column: link_ref[plane, base + part * 9 + row * 3 + column]

    def apply(total, matrix, field, adjoint):
        for row in range(3):
            for column in range(3):
                if adjoint:
                    real, imag = matrix(0, column, row), matrix(1, column, row)
                    total[0][row] += real * field[0][column] + imag * field[1][column]
                    total[1][row] += real * field[1][column] - imag * field[0][column]
                else:
                    real, imag = matrix(0, row, column), matrix(1, row, column)
                    total[0][row] += real * field[0][column] - imag * field[1][column]
                    total[1][row] += real * field[1][column] + imag * field[0][column]

    column_of = lax.broadcasted_iota(jnp.int32, (CHUNK, SITES), 1) % SX
    last, first = column_of == SX - 1, column_of == 0
    pick = pick_ref[0]

    def each(field, change):
        return [[change(field[part][colour]) for colour in range(3)] for part in range(2)]

    def zeros(kind):
        zero = jnp.zeros((CHUNK, SITES), kind)
        return [[zero for _ in range(3)] for _ in range(2)]

    def sweep(plane, here, above, below):
        total = zeros(jnp.bfloat16)
        apply(total, link(plane, 0), each(here, lambda v: ahead_x(v, last)), False)
        apply(total, link(plane, 54), each(here, lambda v: behind_x(v, first)), True)
        apply(total, link(plane, 18), each(here, lambda v: roll_lanes(v, -SX)), False)
        apply(total, link(plane, 72), each(here, lambda v: roll_lanes(v, SX)), True)
        apply(total, link(plane, 36), above, False)
        apply(total, link(plane - 1, 36), below, True)

        def joined(part, colour):
            middle = here[part][colour].astype(jnp.float32)
            change = total[part][colour].astype(jnp.float32) - 6.0 * middle
            return (middle + KAPPA * change).astype(jnp.bfloat16)

        return [[joined(part, colour) for colour in range(3)] for part in range(2)]

    def step(chunk, carry):
        start = pl.multiple_of(chunk * CHUNK, CHUNK)

        def start_field(plane):
            def get(part, colour):
                rows = pl.ds((part * 3 + colour) * HALF + start, CHUNK)
                if plane == 6:
                    return far_ref[rows, :]
                source = (low_ref, mid_ref, high_ref)[plane // 2]
                return source[plane % 2, rows, :]

            return [[get(part, colour) for colour in range(3)] for part in range(2)]

        def stored(ref, plane):
            return [[ref[plane, part * 3 + colour] for colour in range(3)] for part in range(2)]

        for plane in range(1, 6):
            result = sweep(plane, start_field(plane), start_field(plane + 1), start_field(plane - 1))
            for part in range(2):
                for colour in range(3):
                    one_ref[plane, part * 3 + colour] = result[part][colour]
        for plane in range(2, 5):
            result = sweep(plane, stored(one_ref, plane), stored(one_ref, plane + 1), stored(one_ref, plane - 1))
            for part in range(2):
                for colour in range(3):
                    two_ref[plane, part * 3 + colour] = result[part][colour]
        for side in range(2):
            plane = side + 2
            here = each(stored(two_ref, plane), lambda v: v.astype(jnp.float32))
            above = each(stored(two_ref, plane + 1), lambda v: v.astype(jnp.float32))
            incoming = [
                [
                    jnp.where(
                        pick == 0,
                        ahead_x(here[part][colour], last),
                        jnp.where(pick == 1, roll_lanes(here[part][colour], -SX), above[part][colour]),
                    )
                    for colour in range(3)
                ]
                for part in range(2)
            ]
            moved = zeros(jnp.float32)
            chosen = link(plane, pick * 18)
            apply(moved, lambda *at: chosen(*at).astype(jnp.float32), incoming, False)

            def row_of(index):
                return phase_ref[pl.ds(side * 4 + index, 1), :]

            for colour in range(3):

                def put(kind, part, left, real, imag):
                    index = ((kind * 2 + part) * 2 + side) * 3 + colour
                    lanes = pl.ds((index % 2) * SITES, SITES)
                    left_ref[index // 2, pl.ds(start, CHUNK), lanes] = left.astype(jnp.bfloat16)
                    right_ref[index // 2, pl.ds(start, CHUNK), lanes] = real.astype(jnp.bfloat16)
                    right_ref[index // 2, pl.ds(HALF + start, CHUNK), lanes] = imag.astype(jnp.bfloat16)

                def turned(field, base):
                    cosine, sine = row_of(base), row_of(base + 1)
                    return (
                        cosine * field[0][colour] - sine * field[1][colour],
                        cosine * field[1][colour] + sine * field[0][colour],
                    )

                real, imag = turned(moved, 0)
                put(0, 0, here[0][colour], real, imag)
                put(0, 1, here[1][colour], imag, -real)
                real, imag = turned(here, 2)
                put(1, 0, moved[0][colour], real, imag)
                put(1, 1, moved[1][colour], imag, -real)
        return carry

    lax.fori_loop(0, HALF // CHUNK, step, 0)


def smear(pick, phase, low, mid, high, far):
    return pl.pallas_call(
        smear_kernel,
        out_shape=(
            jax.ShapeDtypeStruct((12, HALF, 2 * SITES), jnp.bfloat16),
            jax.ShapeDtypeStruct((12, 2 * HALF, 2 * SITES), jnp.bfloat16),
        ),
        in_specs=[scalar(), whole(), whole(), whole(), whole(), whole()],
        out_specs=(whole(), whole()),
        scratch_shapes=[
            pltpu.VMEM((6, 90, CHUNK, SITES), jnp.bfloat16),
            pltpu.VMEM((6, 6, CHUNK, SITES), jnp.bfloat16),
            pltpu.VMEM((5, 6, CHUNK, SITES), jnp.bfloat16),
        ],
        name="smear",
    )(pick, phase, low, mid, high, far)


def product(left_ref, right_ref):
    total = jnp.zeros((HALF, 2 * HALF), jnp.float32)
    for index in range(12):
        total += lax.dot_general(
            left_ref[index], right_ref[index], (((1,), (1,)), ((), ())), preferred_element_type=jnp.float32
        )
    return total.astype(jnp.bfloat16)


def own_kernel(left_ref, right_ref, out_ref):
    out_ref[...] = product(left_ref, right_ref)


def own_pair(left, right):
    return pl.pallas_call(
        own_kernel,
        out_shape=jax.ShapeDtypeStruct((HALF, 2 * HALF), jnp.bfloat16),
        in_specs=[whole(), whole()],
        out_specs=whole(),
        cost_estimate=pl.CostEstimate(flops=2 * 12 * HALF * 2 * HALF * 2 * SITES, bytes_accessed=3 * 2**20, transcendentals=0),
        name="own_pair",
    )(left, right)


def both_kernel(core_ref, own_ref, left_ref, right_ref, out_ref):
    core = core_ref[0]
    out_ref[pl.ds(pl.multiple_of(core * HALF, HALF), HALF), :] = own_ref[...]
    out_ref[pl.ds(pl.multiple_of((1 - core) * HALF, HALF), HALF), :] = product(left_ref, right_ref)


def both_pair(core, own, left, right):
    return pl.pallas_call(
        both_kernel,
        out_shape=jax.ShapeDtypeStruct((NV, 2 * HALF), jnp.bfloat16),
        in_specs=[scalar(), whole(), whole(), whole()],
        out_specs=whole(),
        name="both_pair",
    )(core, own, left, right)


def spread_kernel(level_ref, source_ref, gathered_ref, out_ref):
    slots = source_ref.shape[0]
    for core in range(2):
        own = gathered_ref[level_ref[0] * 2 + core]
        for slot in range(slots):
            out_ref[core * slots + slot, 0] = own
            out_ref[core * slots + slot, 1] = gathered_ref[source_ref[slot]]


def spread(level, source_list, gathered):
    rows = gathered.shape[1]
    return pl.pallas_call(
        spread_kernel,
        out_shape=jax.ShapeDtypeStruct((2 * source_list.shape[0], 2, rows, 2 * HALF), jnp.bfloat16),
        in_specs=[scalar(), scalar(), whole()],
        out_specs=whole(),
        name="spread",
    )(level, source_list, gathered)


def trace_kernel(arrived_ref, block_ref, out_ref, left_ref, source_ref):
    shares, rows = arrived_ref.shape[0] // 2, arrived_ref.shape[2]
    for share in range(shares):
        at = pl.ds(share * rows, rows)
        below = pl.ds(NV + share * rows, rows)
        for half in range(2):
            for part in range(2):
                lanes = pl.ds(part * NV + half * HALF, HALF)
                source_ref[at, lanes] = arrived_ref[half * shares + share, 1, :, pl.ds(part * HALF, HALF)]
            real = arrived_ref[half * shares + share, 0, :, pl.ds(0, HALF)]
            imag = arrived_ref[half * shares + share, 0, :, pl.ds(HALF, HALF)]
            here, there = pl.ds(half * HALF, HALF), pl.ds(NV + half * HALF, HALF)
            left_ref[at, here] = real
            left_ref[at, there] = -imag
            left_ref[below, here] = imag
            left_ref[below, there] = real

    def folded(value):
        return jnp.sum(value.reshape(NV // 8, 8, NV), axis=0)

    totals = [jnp.zeros((8, NV), jnp.float32)] * 2
    for index in range(block_ref.shape[0]):
        block = block_ref[index]
        first = jnp.dot(left_ref[...], block, preferred_element_type=jnp.float32).astype(jnp.bfloat16)
        second = jnp.dot(first, source_ref[...], preferred_element_type=jnp.float32)
        second_real = second[:NV, :NV] - second[NV:, NV:]
        second_imag = second[:NV, NV:] + second[NV:, :NV]
        block_real = block[:NV].astype(jnp.float32)
        block_imag = block[NV:].astype(jnp.float32)
        totals = [
            totals[0] + folded(second_real * block_real + second_imag * block_imag),
            totals[1] + folded(second_imag * block_real - second_real * block_imag),
        ]
    lane = lax.broadcasted_iota(jnp.int32, out_ref.shape, 1)
    out_ref[...] = jnp.where(lane == 0, jnp.sum(totals[0]), jnp.sum(totals[1]))


def trace(arrived, blocks, copies):
    return pl.pallas_call(
        trace_kernel,
        out_shape=jax.ShapeDtypeStruct((copies, 128), jnp.float32),
        in_specs=[whole(), whole()],
        out_specs=whole(),
        scratch_shapes=[pltpu.VMEM((2 * NV, 2 * NV), jnp.bfloat16), pltpu.VMEM((NV, 2 * NV), jnp.bfloat16)],
        name="trace",
    )(arrived, blocks)


def phases(momentum, pick, pair_index, extent):
    site = jnp.arange(SITES)
    column = (site % SX).astype(jnp.float32)
    row = (site // SX).astype(jnp.float32)
    moment = momentum.astype(jnp.float32)
    height = (pair_index * 2 + jnp.arange(2)).astype(jnp.float32)
    angle = (
        2.0
        * math.pi
        * (moment[0] * column[None] / SX + moment[1] * row[None] / SY + moment[2] * height[:, None] / extent)
    )
    step = jnp.where(pick == 0, moment[0] / SX, jnp.where(pick == 1, moment[1] / SY, moment[2] / extent))
    shifted = angle + 2.0 * math.pi * step
    return jnp.stack([jnp.cos(angle), -jnp.sin(angle), -jnp.cos(shifted), jnp.sin(shifted)], axis=1).reshape(8, SITES)


def per_device(vectors, gauge_links, perambulator, directions, momentum, source_list):
    core = lax.axis_index("core")
    level = lax.axis_index("zh")
    pair_index = lax.axis_index(XY)
    pairs = lax.axis_size(XY)
    rows = NV // pairs

    halves = jnp.swapaxes(vectors[0, :, 0].reshape(6, 2, HALF, SITES), 0, 1).reshape(2, VROWS, SITES)
    link_rows = gauge_links[0, :, :, 0].reshape(54, SITES).astype(jnp.bfloat16)
    pick_row = jnp.broadcast_to(directions[0].astype(jnp.bfloat16), (LROWS - 54, SITES))
    tail = jnp.concatenate([link_rows, pick_row], axis=0)
    plane = jnp.concatenate([halves, jnp.broadcast_to(tail[None], (2, LROWS, SITES))], axis=1)
    crossed = lax.ppermute(plane, ("core", "zh"), [(1, 0), (2, 3)])
    even = level == 0

    def both_planes(index):
        near = lax.dynamic_index_in_dim(plane, index, 0, keepdims=False)
        away = lax.dynamic_index_in_dim(crossed, index, 0, keepdims=False)
        return jnp.stack([jnp.where(even, near, away), jnp.where(even, away, near)])

    taken = lax.ppermute(both_planes(1 - core), ("core", "zh"), [(0, 2), (3, 1)])
    mid = jnp.where(core == level, both_planes(core), taken)

    def moved(value, distance):
        return lax.ppermute(value, XY, [(i, (i + distance) % pairs) for i in range(pairs)])

    high = moved(mid, -1)
    low = moved(mid, 1)
    far = moved(mid[0, :VROWS], -2)
    pick = mid[0, VROWS + 54, 0].astype(jnp.int32)
    phase = phases(momentum, pick, pair_index, 2 * pairs)
    left, right = smear(pick[None], phase, low, mid, high, far)
    other = lax.ppermute(left, "core", [(0, 1), (1, 0)])
    partial_value = both_pair(core[None], own_pair(left, right), other, right)

    parts = lax.all_to_all(partial_value, XY, 0, 0, tiled=True).reshape(pairs, rows, 2 * HALF)
    scale = 1.0 / math.sqrt(3 * SITES * 2 * pairs)
    share = (jnp.sum(parts.astype(jnp.float32), axis=0) * scale).astype(jnp.bfloat16)

    slices = lax.axis_size(("zl", "zh"))
    copies = jnp.broadcast_to(share[None], (slices, rows, 2 * HALF))
    gathered = lax.all_to_all(copies, ("zl", "zh"), 0, 0, tiled=True)
    sent = spread(lax.axis_index("zl")[None], source_list, gathered)
    arrived = lax.all_to_all(sent, ("core", "y", "x"), 0, 0, tiled=True)

    space_count = lax.axis_size(SPACE)
    blocks = perambulator[0].reshape(-1, 2 * NV, NV)
    value = trace(arrived, blocks, space_count)
    values = lax.all_to_all(value, SPACE, 0, 0, tiled=True)[:, :2].reshape(pairs, 2, 2)
    per_slot = jnp.sum(values, axis=1) / (NS * NV)
    one_hot = (source_list[:, None] == jnp.arange(source_list.shape[0])[None]).astype(jnp.float32)
    correlator = jnp.sum(per_slot[:, :, None] * one_hot[:, None, :], axis=0)

    own_rows = NV // space_count
    mine = lax.dynamic_index_in_dim(arrived.reshape(2, pairs, 2, rows, 2, HALF)[:, :, 0], pair_index, 1, keepdims=False)
    mine = lax.dynamic_slice_in_dim(mine, level * own_rows, own_rows, 1)
    elemental = jnp.transpose(mine, (1, 2, 0, 3)).reshape(1, own_rows, 2, NV)
    return elemental, correlator[:, None, :]


def solution(mesh):
    grid = Mesh(mesh.devices.reshape(8, 2, 4, 4, 2), ("zl", "core", "y", "x", "zh"))
    times = ("zl", "core")
    in_specs = (
        P(times, None, SPACE, None, None, None),
        P(times, None, None, SPACE, None, None, None),
        P(times, SPACE, None, None, None),
        P(times),
        P(),
        P(),
    )
    out_specs = (P(times, SPACE, None, None), P(None, times, None))
    return jax.shard_map(per_device, mesh=grid, in_specs=in_specs, out_specs=out_specs, check_vma=False)
```

```python
import math

import jax
import jax.numpy as jnp
from jax import lax
from jax.experimental import pallas as pl
from jax.experimental.pallas import tpu as pltpu
from jax.sharding import Mesh, PartitionSpec as P


NV = 256
NS = 4
SX = 16
SY = 8
SITES = SX * SY
HALF = NV // 2
VROWS = 6 * HALF
LROWS = 64
KAPPA = 0.05

SPACE = ("y", "x", "zh")
XY = ("y", "x")
CHUNK = 16


def whole():
    return pl.BlockSpec(memory_space=pltpu.VMEM)


def scalar():
    return pl.BlockSpec(memory_space=pltpu.SMEM)


def roll_lanes(value, shift):
    return pltpu.roll(value, shift % SITES, value.ndim - 1)


def ahead_x(value, last):
    return jnp.where(last, roll_lanes(value, SX - 1), roll_lanes(value, -1))


def behind_x(value, first):
    return jnp.where(first, roll_lanes(value, 1 - SX), roll_lanes(value, 1))


def smear_kernel(pick_ref, level_ref, phase_ref, *refs):
    low, mid, high, far = refs[0:2], refs[2:4], refs[4:6], refs[6:8]
    left_ref, right_ref, link_ref, field_ref, one_ref, two_ref = refs[8:]

    def load(even):
        for index, group in enumerate((low, mid, high)):
            for parity in range(2):
                source = group[parity if even else 1 - parity]
                field_ref[index * 2 + parity] = source[pl.ds(0, VROWS), :].astype(jnp.float32)
                link_ref[index * 2 + parity, pl.ds(0, LROWS), :] = source[pl.ds(VROWS, LROWS), :].astype(jnp.float32)
        field_ref[6] = far[0 if even else 1][...].astype(jnp.float32)

    @pl.when(level_ref[0] == 0)
    def _():
        load(True)

    @pl.when(level_ref[0] != 0)
    def _():
        load(False)

    site = lax.broadcasted_iota(jnp.int32, (18, SITES), 1) % SX
    for plane in range(1, 6):
        link_ref[plane, pl.ds(64, 18), :] = behind_x(link_ref[plane, pl.ds(0, 18), :], site == 0)
        link_ref[plane, pl.ds(88, 18), :] = roll_lanes(link_ref[plane, pl.ds(18, 18), :], SX)

    def link(plane, base):
        def get(part, row, column):
            line = link_ref[plane, pl.ds(base + part * 9 + row * 3 + column, 1), :]
            return jnp.broadcast_to(line, (CHUNK, SITES))

        return get

    def packed(matrix):
        return lambda *at: matrix(*at).astype(jnp.bfloat16)

    def apply(total, matrix, field, adjoint):
        for row in range(3):
            for column in range(3):
                if adjoint:
                    real, imag = matrix(0, column, row), matrix(1, column, row)
                    total[0][row] += real * field[0][column] + imag * field[1][column]
                    total[1][row] += real * field[1][column] - imag * field[0][column]
                else:
                    real, imag = matrix(0, row, column), matrix(1, row, column)
                    total[0][row] += real * field[0][column] - imag * field[1][column]
                    total[1][row] += real * field[1][column] + imag * field[0][column]

    column_of = lax.broadcasted_iota(jnp.int32, (CHUNK, SITES), 1) % SX
    last, first = column_of == SX - 1, column_of == 0
    pick = pick_ref[0]

    def each(field, change):
        return [[change(field[part][colour]) for colour in range(3)] for part in range(2)]

    def zeros(kind):
        zero = jnp.zeros((CHUNK, SITES), kind)
        return [[zero for _ in range(3)] for _ in range(2)]

    def narrow(field):
        return each(field, lambda v: v.astype(jnp.bfloat16))

    def sweep(plane, here, above, below):
        total = zeros(jnp.bfloat16)
        middle = narrow(here)
        apply(total, packed(link(plane, 0)), each(middle, lambda v: ahead_x(v, last)), False)
        apply(total, packed(link(plane, 64)), each(middle, lambda v: behind_x(v, first)), True)
        apply(total, packed(link(plane, 18)), each(middle, lambda v: roll_lanes(v, -SX)), False)
        apply(total, packed(link(plane, 88)), each(middle, lambda v: roll_lanes(v, SX)), True)
        apply(total, packed(link(plane, 36)), narrow(above), False)
        apply(total, packed(link(plane - 1, 36)), narrow(below), True)

        def joined(part, colour):
            return (1.0 - 6.0 * KAPPA) * here[part][colour] + KAPPA * total[part][colour].astype(jnp.float32)

        return [[joined(part, colour) for colour in range(3)] for part in range(2)]

    def step(chunk, carry):
        start = pl.multiple_of(chunk * CHUNK, CHUNK)

        def start_field(plane):
            return [
                [field_ref[plane, pl.ds((part * 3 + colour) * HALF + start, CHUNK), :] for colour in range(3)]
                for part in range(2)
            ]

        def stored(ref, plane):
            return [[ref[plane, part * 3 + colour] for colour in range(3)] for part in range(2)]

        for plane in range(1, 6):
            result = sweep(plane, start_field(plane), start_field(plane + 1), start_field(plane - 1))
            for part in range(2):
                for colour in range(3):
                    one_ref[plane, part * 3 + colour] = result[part][colour]
        for plane in range(2, 5):
            result = sweep(plane, stored(one_ref, plane), stored(one_ref, plane + 1), stored(one_ref, plane - 1))
            for part in range(2):
                for colour in range(3):
                    two_ref[plane, part * 3 + colour] = result[part][colour]
        for side in range(2):
            plane = side + 2
            here, above = stored(two_ref, plane), stored(two_ref, plane + 1)
            incoming = [
                [
                    jnp.where(
                        pick == 0,
                        ahead_x(here[part][colour], last),
                        jnp.where(pick == 1, roll_lanes(here[part][colour], -SX), above[part][colour]),
                    )
                    for colour in range(3)
                ]
                for part in range(2)
            ]
            moved = zeros(jnp.float32)
            apply(moved, link(plane, pick * 18), incoming, False)

            def row_of(index):
                return phase_ref[pl.ds(side * 4 + index, 1), :]

            for colour in range(3):

                def put(kind, part, left, real, imag):
                    index = ((kind * 2 + part) * 2 + side) * 3 + colour
                    lanes = pl.ds((index % 2) * SITES, SITES)
                    left_ref[index // 2, pl.ds(start, CHUNK), lanes] = left.astype(jnp.bfloat16)
                    right_ref[index // 2, pl.ds(start, CHUNK), lanes] = real.astype(jnp.bfloat16)
                    right_ref[index // 2, pl.ds(HALF + start, CHUNK), lanes] = imag.astype(jnp.bfloat16)

                def turned(field, base):
                    cosine, sine = row_of(base), row_of(base + 1)
                    return (
                        cosine * field[0][colour] - sine * field[1][colour],
                        cosine * field[1][colour] + sine * field[0][colour],
                    )

                real, imag = turned(moved, 0)
                put(0, 0, here[0][colour], real, imag)
                put(0, 1, here[1][colour], imag, -real)
                real, imag = turned(here, 2)
                put(1, 0, moved[0][colour], real, imag)
                put(1, 1, moved[1][colour], imag, -real)
        return carry

    lax.fori_loop(0, HALF // CHUNK, step, 0)


def room(megabytes):
    return pltpu.CompilerParams(vmem_limit_bytes=megabytes * 2**20)


def smear(pick, level, phase, *planes):
    return pl.pallas_call(
        smear_kernel,
        out_shape=(
            jax.ShapeDtypeStruct((12, HALF, 2 * SITES), jnp.bfloat16),
            jax.ShapeDtypeStruct((12, 2 * HALF, 2 * SITES), jnp.bfloat16),
        ),
        in_specs=[scalar(), scalar()] + [whole()] * (1 + len(planes)),
        out_specs=(whole(), whole()),
        scratch_shapes=[
            pltpu.VMEM((6, 112, SITES), jnp.float32),
            pltpu.VMEM((7, VROWS, SITES), jnp.float32),
            pltpu.VMEM((6, 6, CHUNK, SITES), jnp.float32),
            pltpu.VMEM((5, 6, CHUNK, SITES), jnp.float32),
        ],
        compiler_params=room(14),
        name="smear",
    )(pick, level, phase, *planes)


def pair_kernel(core_ref, own_ref, other_ref, right_ref, out_ref):
    core = core_ref[0]

    def product(ref):
        total = jnp.zeros((HALF, 2 * HALF), jnp.float32)
        for index in range(12):
            total += lax.dot_general(
                ref[index], right_ref[index], (((1,), (1,)), ((), ())), preferred_element_type=jnp.float32
            )
        return total.astype(jnp.bfloat16)

    out_ref[pl.ds(pl.multiple_of(core * HALF, HALF), HALF), :] = product(own_ref)
    out_ref[pl.ds(pl.multiple_of((1 - core) * HALF, HALF), HALF), :] = product(other_ref)


def pair(core, own, other, right):
    return pl.pallas_call(
        pair_kernel,
        out_shape=jax.ShapeDtypeStruct((NV, 2 * HALF), jnp.bfloat16),
        in_specs=[scalar(), whole(), whole(), whole()],
        out_specs=whole(),
        compiler_params=room(8),
        name="pair",
    )(core, own, other, right)


def spread_kernel(level_ref, source_ref, gathered_ref, out_ref):
    slots = source_ref.shape[0]
    for core in range(2):
        own = gathered_ref[level_ref[0] * 2 + core]
        for slot in range(slots):
            out_ref[core * slots + slot, 0] = own
            out_ref[core * slots + slot, 1] = gathered_ref[source_ref[slot]]


def spread(level, source_list, gathered):
    rows = gathered.shape[1]
    return pl.pallas_call(
        spread_kernel,
        out_shape=jax.ShapeDtypeStruct((2 * source_list.shape[0], 2, rows, 2 * HALF), jnp.bfloat16),
        in_specs=[scalar(), scalar(), whole()],
        out_specs=whole(),
        compiler_params=room(4),
        name="spread",
    )(level, source_list, gathered)


def trace_kernel(arrived_ref, block_ref, out_ref, left_ref, source_ref):
    shares, rows = arrived_ref.shape[0] // 2, arrived_ref.shape[2]
    for share in range(shares):
        at = pl.ds(share * rows, rows)
        below = pl.ds(NV + share * rows, rows)
        for half in range(2):
            for part in range(2):
                lanes = pl.ds(part * NV + half * HALF, HALF)
                source_ref[at, lanes] = arrived_ref[half * shares + share, 1, :, pl.ds(part * HALF, HALF)]
            real = arrived_ref[half * shares + share, 0, :, pl.ds(0, HALF)]
            imag = arrived_ref[half * shares + share, 0, :, pl.ds(HALF, HALF)]
            here, there = pl.ds(half * HALF, HALF), pl.ds(NV + half * HALF, HALF)
            left_ref[at, here] = real
            left_ref[at, there] = -imag
            left_ref[below, here] = imag
            left_ref[below, there] = real

    def folded(value):
        return jnp.sum(value.reshape(NV // 8, 8, NV), axis=0)

    totals = [jnp.zeros((8, NV), jnp.float32)] * 2
    for index in range(block_ref.shape[0]):
        block = block_ref[index]
        first = jnp.dot(left_ref[...], block, preferred_element_type=jnp.float32).astype(jnp.bfloat16)
        second = jnp.dot(first, source_ref[...], preferred_element_type=jnp.float32)
        second_real = second[:NV, :NV] - second[NV:, NV:]
        second_imag = second[:NV, NV:] + second[NV:, :NV]
        block_real = block[:NV].astype(jnp.float32)
        block_imag = block[NV:].astype(jnp.float32)
        totals = [
            totals[0] + folded(second_real * block_real + second_imag * block_imag),
            totals[1] + folded(second_imag * block_real - second_real * block_imag),
        ]
    lane = lax.broadcasted_iota(jnp.int32, out_ref.shape, 1)
    out_ref[...] = jnp.where(lane == 0, jnp.sum(totals[0]), jnp.sum(totals[1]))


def trace(arrived, blocks, copies):
    return pl.pallas_call(
        trace_kernel,
        out_shape=jax.ShapeDtypeStruct((copies, 128), jnp.float32),
        in_specs=[whole(), whole()],
        out_specs=whole(),
        scratch_shapes=[pltpu.VMEM((2 * NV, 2 * NV), jnp.bfloat16), pltpu.VMEM((NV, 2 * NV), jnp.bfloat16)],
        compiler_params=room(12),
        name="trace",
    )(arrived, blocks)


def phases(momentum, pick, pair_index, extent):
    site = jnp.arange(SITES)
    column = (site % SX).astype(jnp.float32)
    row = (site // SX).astype(jnp.float32)
    moment = momentum.astype(jnp.float32)
    height = (pair_index * 2 + jnp.arange(2)).astype(jnp.float32)
    angle = (
        2.0
        * math.pi
        * (moment[0] * column[None] / SX + moment[1] * row[None] / SY + moment[2] * height[:, None] / extent)
    )
    step = jnp.where(pick == 0, moment[0] / SX, jnp.where(pick == 1, moment[1] / SY, moment[2] / extent))
    shifted = angle + 2.0 * math.pi * step
    return jnp.stack([jnp.cos(angle), -jnp.sin(angle), -jnp.cos(shifted), jnp.sin(shifted)], axis=1).reshape(8, SITES)


def per_device(vectors, gauge_links, perambulator, directions, momentum, source_list):
    core = lax.axis_index("core")
    level = lax.axis_index("zh")
    pair_index = lax.axis_index(XY)
    pairs = lax.axis_size(XY)
    rows = NV // pairs

    links = gauge_links[0, :, :, 0].reshape(54, SITES).astype(jnp.bfloat16)
    pick_row = jnp.broadcast_to(directions[0].astype(jnp.bfloat16), (LROWS - 54, SITES))
    tail = jnp.concatenate([links, pick_row], axis=0)
    own_vectors = vectors[0, :, 0].reshape(6, NV, SITES)
    sites = ("core", "zh")
    cross_vectors = lax.ppermute(own_vectors, sites, [(1, 0), (2, 3)])
    cross_tail = lax.ppermute(tail, sites, [(1, 0), (2, 3)])
    same = core == level

    def share_out(planes, rows_of_links):
        def half_of(index):
            half = lax.dynamic_slice_in_dim(planes, index * HALF, HALF, 1).reshape(VROWS, SITES)
            return jnp.concatenate([half, rows_of_links], axis=0)

        taken = lax.ppermute(half_of(1 - core), sites, [(0, 2), (3, 1)])
        return jnp.where(same, half_of(core), taken)

    def moved(value, distance, levels):
        route = [(i * 2 + z, (i + distance) % pairs * 2 + z) for i in range(pairs) for z in levels]
        return lax.ppermute(value, SPACE, route)

    def around(plane, far_levels):
        low, high = moved(plane, 1, (0, 1)), moved(plane, -1, (0, 1))
        return low, plane, high, moved(plane[:VROWS], -2, far_levels)

    own = around(share_out(own_vectors, tail), (0,))
    own, cross_vectors, cross_tail = lax.optimization_barrier((own, cross_vectors, cross_tail))
    other = around(share_out(cross_vectors, cross_tail), (1,))
    pick = own[1][VROWS + 54, 0].astype(jnp.int32)
    phase = phases(momentum, pick, pair_index, 2 * pairs)
    planes = [plane for couple in zip(own, other) for plane in couple]
    left, right = smear(pick[None], level[None], phase, *planes)
    sibling = lax.ppermute(left, "core", [(0, 1), (1, 0)])
    partial_value = pair(core[None], left, sibling, right)

    parts = lax.all_to_all(partial_value, XY, 0, 0, tiled=True).reshape(pairs, rows, 2 * HALF)
    scale = 1.0 / math.sqrt(3 * SITES * 2 * pairs)
    share = (jnp.sum(parts.astype(jnp.float32), axis=0) * scale).astype(jnp.bfloat16)

    slices = lax.axis_size(("zl", "zh"))
    copies = jnp.broadcast_to(share[None], (slices, rows, 2 * HALF))
    gathered = lax.all_to_all(copies, ("zl", "zh"), 0, 0, tiled=True)
    sent = spread(lax.axis_index("zl")[None], source_list, gathered)
    arrived = lax.all_to_all(sent, ("core", "y", "x"), 0, 0, tiled=True)

    space_count = lax.axis_size(SPACE)
    blocks = perambulator[0].reshape(-1, 2 * NV, NV)
    value = trace(arrived, blocks, space_count)
    values = lax.all_to_all(value, SPACE, 0, 0, tiled=True)[:, :2].reshape(pairs, 2, 2)
    per_slot = jnp.sum(values, axis=1) / (NS * NV)
    one_hot = (source_list[:, None] == jnp.arange(source_list.shape[0])[None]).astype(jnp.float32)
    correlator = jnp.sum(per_slot[:, :, None] * one_hot[:, None, :], axis=0)

    own_rows = NV // space_count
    mine = lax.dynamic_index_in_dim(arrived.reshape(2, pairs, 2, rows, 2, HALF)[:, :, 0], pair_index, 1, keepdims=False)
    mine = lax.dynamic_slice_in_dim(mine, level * own_rows, own_rows, 1)
    elemental = jnp.transpose(mine, (1, 2, 0, 3)).reshape(1, own_rows, 2, NV)
    return elemental, correlator[:, None, :]


def solution(mesh):
    grid = Mesh(mesh.devices.reshape(8, 2, 4, 4, 2), ("zl", "core", "y", "x", "zh"))
    times = ("zl", "core")
    in_specs = (
        P(times, None, SPACE, None, None, None),
        P(times, None, None, SPACE, None, None, None),
        P(times, SPACE, None, None, None),
        P(times),
        P(),
        P(),
    )
    out_specs = (P(times, SPACE, None, None), P(None, times, None))

    return jax.shard_map(per_device, mesh=grid, in_specs=in_specs, out_specs=out_specs, check_vma=False)
```

```python
import math

import jax
import jax.numpy as jnp
from jax import lax
from jax.experimental import pallas as pl
from jax.experimental.pallas import tpu as pltpu
from jax.sharding import Mesh, PartitionSpec as P


NV = 256
NS = 4
SX = 16
SY = 8
SITES = SX * SY
HALF = NV // 2
VROWS = 6 * HALF
LROWS = 64
KAPPA = 0.05

SPACE = ("y", "x", "zh")
XY = ("y", "x")
CHUNK = 16


def whole():
    return pl.BlockSpec(memory_space=pltpu.VMEM)


def scalar():
    return pl.BlockSpec(memory_space=pltpu.SMEM)


def roll_lanes(value, shift):
    return pltpu.roll(value, shift % SITES, value.ndim - 1)


def ahead_x(value, last):
    return jnp.where(last, roll_lanes(value, SX - 1), roll_lanes(value, -1))


def behind_x(value, first):
    return jnp.where(first, roll_lanes(value, 1 - SX), roll_lanes(value, 1))


def smear_kernel(pick_ref, level_ref, phase_ref, *refs):
    low, mid, high, far = refs[0:2], refs[2:4], refs[4:6], refs[6:8]
    left_ref, right_ref, link_ref, field_ref, one_ref, two_ref = refs[8:]

    def load(even):
        for index, group in enumerate((low, mid, high)):
            for parity in range(2):
                source = group[parity if even else 1 - parity]
                field_ref[index * 2 + parity] = source[pl.ds(0, VROWS), :].astype(jnp.float32)
                link_ref[index * 2 + parity, pl.ds(0, LROWS), :] = source[pl.ds(VROWS, LROWS), :].astype(jnp.float32)
        field_ref[6] = far[0 if even else 1][...].astype(jnp.float32)

    @pl.when(level_ref[0] == 0)
    def _():
        load(True)

    @pl.when(level_ref[0] != 0)
    def _():
        load(False)

    site = lax.broadcasted_iota(jnp.int32, (18, SITES), 1) % SX
    for plane in range(1, 6):
        link_ref[plane, pl.ds(64, 18), :] = behind_x(link_ref[plane, pl.ds(0, 18), :], site == 0)
        link_ref[plane, pl.ds(88, 18), :] = roll_lanes(link_ref[plane, pl.ds(18, 18), :], SX)

    def link(plane, base):
        def get(part, row, column):
            line = link_ref[plane, pl.ds(base + part * 9 + row * 3 + column, 1), :]
            return jnp.broadcast_to(line, (CHUNK, SITES))

        return get

    def packed(matrix):
        return lambda *at: matrix(*at).astype(jnp.bfloat16)

    def apply(total, matrix, field, adjoint):
        for row in range(3):
            for column in range(3):
                if adjoint:
                    real, imag = matrix(0, column, row), matrix(1, column, row)
                    total[0][row] += real * field[0][column] + imag * field[1][column]
                    total[1][row] += real * field[1][column] - imag * field[0][column]
                else:
                    real, imag = matrix(0, row, column), matrix(1, row, column)
                    total[0][row] += real * field[0][column] - imag * field[1][column]
                    total[1][row] += real * field[1][column] + imag * field[0][column]

    column_of = lax.broadcasted_iota(jnp.int32, (CHUNK, SITES), 1) % SX
    last, first = column_of == SX - 1, column_of == 0
    pick = pick_ref[0]

    def each(field, change):
        return [[change(field[part][colour]) for colour in range(3)] for part in range(2)]

    def zeros(kind):
        zero = jnp.zeros((CHUNK, SITES), kind)
        return [[zero for _ in range(3)] for _ in range(2)]

    def narrow(field):
        return each(field, lambda v: v.astype(jnp.bfloat16))

    def sweep(plane, here, above, below):
        total = zeros(jnp.bfloat16)
        middle = narrow(here)
        apply(total, packed(link(plane, 0)), each(middle, lambda v: ahead_x(v, last)), False)
        apply(total, packed(link(plane, 64)), each(middle, lambda v: behind_x(v, first)), True)
        apply(total, packed(link(plane, 18)), each(middle, lambda v: roll_lanes(v, -SX)), False)
        apply(total, packed(link(plane, 88)), each(middle, lambda v: roll_lanes(v, SX)), True)
        apply(total, packed(link(plane, 36)), narrow(above), False)
        apply(total, packed(link(plane - 1, 36)), narrow(below), True)

        def joined(part, colour):
            return (1.0 - 6.0 * KAPPA) * here[part][colour] + KAPPA * total[part][colour].astype(jnp.float32)

        return [[joined(part, colour) for colour in range(3)] for part in range(2)]

    def step(chunk, carry):
        start = pl.multiple_of(chunk * CHUNK, CHUNK)

        def start_field(plane):
            return [
                [field_ref[plane, pl.ds((part * 3 + colour) * HALF + start, CHUNK), :] for colour in range(3)]
                for part in range(2)
            ]

        def stored(ref, plane):
            return [[ref[plane, part * 3 + colour] for colour in range(3)] for part in range(2)]

        for plane in range(1, 6):
            result = sweep(plane, start_field(plane), start_field(plane + 1), start_field(plane - 1))
            for part in range(2):
                for colour in range(3):
                    one_ref[plane, part * 3 + colour] = result[part][colour]
        for plane in range(2, 5):
            result = sweep(plane, stored(one_ref, plane), stored(one_ref, plane + 1), stored(one_ref, plane - 1))
            for part in range(2):
                for colour in range(3):
                    two_ref[plane, part * 3 + colour] = result[part][colour]
        for side in range(2):
            plane = side + 2
            here, above = stored(two_ref, plane), stored(two_ref, plane + 1)
            incoming = [
                [
                    jnp.where(
                        pick == 0,
                        ahead_x(here[part][colour], last),
                        jnp.where(pick == 1, roll_lanes(here[part][colour], -SX), above[part][colour]),
                    )
                    for colour in range(3)
                ]
                for part in range(2)
            ]
            moved = zeros(jnp.float32)
            apply(moved, link(plane, pick * 18), incoming, False)

            def row_of(index):
                return phase_ref[pl.ds(side * 4 + index, 1), :]

            for colour in range(3):

                def put(kind, part, left, real, imag):
                    index = ((kind * 2 + part) * 2 + side) * 3 + colour
                    lanes = pl.ds((index % 2) * SITES, SITES)
                    left_ref[index // 2, pl.ds(start, CHUNK), lanes] = left.astype(jnp.bfloat16)
                    right_ref[index // 2, pl.ds(start, CHUNK), lanes] = real.astype(jnp.bfloat16)
                    right_ref[index // 2, pl.ds(HALF + start, CHUNK), lanes] = imag.astype(jnp.bfloat16)

                def turned(field, base):
                    cosine, sine = row_of(base), row_of(base + 1)
                    return (
                        cosine * field[0][colour] - sine * field[1][colour],
                        cosine * field[1][colour] + sine * field[0][colour],
                    )

                real, imag = turned(moved, 0)
                put(0, 0, here[0][colour], real, imag)
                put(0, 1, here[1][colour], imag, -real)
                real, imag = turned(here, 2)
                put(1, 0, moved[0][colour], real, imag)
                put(1, 1, moved[1][colour], imag, -real)
        return carry

    lax.fori_loop(0, HALF // CHUNK, step, 0)


def room(megabytes):
    return pltpu.CompilerParams(vmem_limit_bytes=megabytes * 2**20)


def smear(pick, level, phase, *planes):
    return pl.pallas_call(
        smear_kernel,
        out_shape=(
            jax.ShapeDtypeStruct((12, HALF, 2 * SITES), jnp.bfloat16),
            jax.ShapeDtypeStruct((12, 2 * HALF, 2 * SITES), jnp.bfloat16),
        ),
        in_specs=[scalar(), scalar()] + [whole()] * (1 + len(planes)),
        out_specs=(whole(), whole()),
        scratch_shapes=[
            pltpu.VMEM((6, 112, SITES), jnp.float32),
            pltpu.VMEM((7, VROWS, SITES), jnp.float32),
            pltpu.VMEM((6, 6, CHUNK, SITES), jnp.float32),
            pltpu.VMEM((5, 6, CHUNK, SITES), jnp.float32),
        ],
        compiler_params=room(14),
        name="smear",
    )(pick, level, phase, *planes)


def pair_kernel(core_ref, own_ref, other_ref, right_ref, out_ref):
    core = core_ref[0]

    def product(ref):
        total = jnp.zeros((HALF, 2 * HALF), jnp.float32)
        for index in range(12):
            total += lax.dot_general(
                ref[index], right_ref[index], (((1,), (1,)), ((), ())), preferred_element_type=jnp.float32
            )
        return total.astype(jnp.bfloat16)

    out_ref[pl.ds(pl.multiple_of(core * HALF, HALF), HALF), :] = product(own_ref)
    out_ref[pl.ds(pl.multiple_of((1 - core) * HALF, HALF), HALF), :] = product(other_ref)


def pair(core, own, other, right):
    return pl.pallas_call(
        pair_kernel,
        out_shape=jax.ShapeDtypeStruct((NV, 2 * HALF), jnp.bfloat16),
        in_specs=[scalar(), whole(), whole(), whole()],
        out_specs=whole(),
        compiler_params=room(8),
        name="pair",
    )(core, own, other, right)


def spread_kernel(level_ref, source_ref, gathered_ref, out_ref):
    slots = source_ref.shape[0]
    for core in range(2):
        own = gathered_ref[level_ref[0] * 2 + core]
        for slot in range(slots):
            out_ref[core * slots + slot, 0] = own
            out_ref[core * slots + slot, 1] = gathered_ref[source_ref[slot]]


def spread(level, source_list, gathered):
    rows = gathered.shape[1]
    return pl.pallas_call(
        spread_kernel,
        out_shape=jax.ShapeDtypeStruct((2 * source_list.shape[0], 2, rows, 2 * HALF), jnp.bfloat16),
        in_specs=[scalar(), scalar(), whole()],
        out_specs=whole(),
        compiler_params=room(4),
        name="spread",
    )(level, source_list, gathered)


def trace_kernel(arrived_ref, block_ref, out_ref, left_ref, source_ref):
    shares, rows = arrived_ref.shape[0] // 2, arrived_ref.shape[2]
    for share in range(shares):
        at = pl.ds(share * rows, rows)
        below = pl.ds(NV + share * rows, rows)
        for half in range(2):
            for part in range(2):
                lanes = pl.ds(part * NV + half * HALF, HALF)
                source_ref[at, lanes] = arrived_ref[half * shares + share, 1, :, pl.ds(part * HALF, HALF)]
            real = arrived_ref[half * shares + share, 0, :, pl.ds(0, HALF)]
            imag = arrived_ref[half * shares + share, 0, :, pl.ds(HALF, HALF)]
            here, there = pl.ds(half * HALF, HALF), pl.ds(NV + half * HALF, HALF)
            left_ref[at, here] = real
            left_ref[at, there] = -imag
            left_ref[below, here] = imag
            left_ref[below, there] = real

    def folded(value):
        return jnp.sum(value.reshape(NV // 8, 8, NV), axis=0)

    totals = [jnp.zeros((8, NV), jnp.float32)] * 2
    for index in range(block_ref.shape[0]):
        block = block_ref[index]
        first = jnp.dot(left_ref[...], block, preferred_element_type=jnp.float32).astype(jnp.bfloat16)
        second = jnp.dot(first, source_ref[...], preferred_element_type=jnp.float32)
        second_real = second[:NV, :NV] - second[NV:, NV:]
        second_imag = second[:NV, NV:] + second[NV:, :NV]
        block_real = block[:NV].astype(jnp.float32)
        block_imag = block[NV:].astype(jnp.float32)
        totals = [
            totals[0] + folded(second_real * block_real + second_imag * block_imag),
            totals[1] + folded(second_imag * block_real - second_real * block_imag),
        ]
    lane = lax.broadcasted_iota(jnp.int32, out_ref.shape, 1)
    out_ref[...] = jnp.where(lane == 0, jnp.sum(totals[0]), jnp.sum(totals[1]))


def trace(arrived, blocks, copies):
    return pl.pallas_call(
        trace_kernel,
        out_shape=jax.ShapeDtypeStruct((copies, 128), jnp.float32),
        in_specs=[whole(), whole()],
        out_specs=whole(),
        scratch_shapes=[pltpu.VMEM((2 * NV, 2 * NV), jnp.bfloat16), pltpu.VMEM((NV, 2 * NV), jnp.bfloat16)],
        compiler_params=room(12),
        name="trace",
    )(arrived, blocks)


def phases(momentum, pick, pair_index, extent):
    site = jnp.arange(SITES)
    column = (site % SX).astype(jnp.float32)
    row = (site // SX).astype(jnp.float32)
    moment = momentum.astype(jnp.float32)
    height = (pair_index * 2 + jnp.arange(2)).astype(jnp.float32)
    angle = (
        2.0
        * math.pi
        * (moment[0] * column[None] / SX + moment[1] * row[None] / SY + moment[2] * height[:, None] / extent)
    )
    step = jnp.where(pick == 0, moment[0] / SX, jnp.where(pick == 1, moment[1] / SY, moment[2] / extent))
    shifted = angle + 2.0 * math.pi * step
    return jnp.stack([jnp.cos(angle), -jnp.sin(angle), -jnp.cos(shifted), jnp.sin(shifted)], axis=1).reshape(8, SITES)


def per_device(vectors, gauge_links, perambulator, directions, momentum, source_list):
    core = lax.axis_index("core")
    level = lax.axis_index("zh")
    pair_index = lax.axis_index(XY)
    pairs = lax.axis_size(XY)
    rows = NV // pairs

    links = gauge_links[0, :, :, 0].reshape(54, SITES).astype(jnp.bfloat16)
    pick_row = jnp.broadcast_to(directions[0].astype(jnp.bfloat16), (LROWS - 54, SITES))
    tail = jnp.concatenate([links, pick_row], axis=0)
    planes_here = vectors[0, :, 0].reshape(6, NV, SITES)
    sites = ("core", "zh")
    same = core == level

    def half_of(index):
        half = lax.dynamic_slice_in_dim(planes_here, index * HALF, HALF, 1).reshape(VROWS, SITES)
        return jnp.concatenate([half, tail], axis=0)

    first_half, second_half = lax.optimization_barrier((half_of(core), half_of(1 - core)))
    cross_same = lax.ppermute(first_half, sites, [(1, 0), (2, 3)])
    cross_sibling = lax.ppermute(second_half, sites, [(1, 2), (2, 1)])

    def moved(value, distance, levels):
        route = [(i * 2 + z, (i + distance) % pairs * 2 + z) for i in range(pairs) for z in levels]
        return lax.ppermute(value, SPACE, route)

    def around(plane, far_levels):
        low, high = moved(plane, 1, (0, 1)), moved(plane, -1, (0, 1))
        return low, plane, high, moved(plane[:VROWS], -2, far_levels)

    taken = lax.ppermute(second_half, sites, [(0, 2), (3, 1)])
    own = around(jnp.where(same, first_half, taken), (0,))
    own, cross_same, cross_sibling = lax.optimization_barrier((own, cross_same, cross_sibling))
    other = around(jnp.where(same, cross_same, cross_sibling), (1,))
    pick = own[1][VROWS + 54, 0].astype(jnp.int32)
    phase = phases(momentum, pick, pair_index, 2 * pairs)
    planes = [plane for couple in zip(own, other) for plane in couple]
    left, right = smear(pick[None], level[None], phase, *planes)
    sibling = lax.ppermute(left, "core", [(0, 1), (1, 0)])
    partial_value = pair(core[None], left, sibling, right)

    parts = lax.all_to_all(partial_value, XY, 0, 0, tiled=True).reshape(pairs, rows, 2 * HALF)
    scale = 1.0 / math.sqrt(3 * SITES * 2 * pairs)
    share = (jnp.sum(parts.astype(jnp.float32), axis=0) * scale).astype(jnp.bfloat16)

    slices = lax.axis_size(("zl", "zh"))
    copies = jnp.broadcast_to(share[None], (slices, rows, 2 * HALF))
    gathered = lax.all_to_all(copies, ("zl", "zh"), 0, 0, tiled=True)
    sent = spread(lax.axis_index("zl")[None], source_list, gathered)
    arrived = lax.all_to_all(sent, ("core", "y", "x"), 0, 0, tiled=True)

    space_count = lax.axis_size(SPACE)
    blocks = perambulator[0].reshape(-1, 2 * NV, NV)
    value = trace(arrived, blocks, space_count)
    values = lax.all_to_all(value, SPACE, 0, 0, tiled=True)[:, :2].reshape(pairs, 2, 2)
    per_slot = jnp.sum(values, axis=1) / (NS * NV)
    one_hot = (source_list[:, None] == jnp.arange(source_list.shape[0])[None]).astype(jnp.float32)
    correlator = jnp.sum(per_slot[:, :, None] * one_hot[:, None, :], axis=0)

    own_rows = NV // space_count
    mine = lax.dynamic_index_in_dim(arrived.reshape(2, pairs, 2, rows, 2, HALF)[:, :, 0], pair_index, 1, keepdims=False)
    mine = lax.dynamic_slice_in_dim(mine, level * own_rows, own_rows, 1)
    elemental = jnp.transpose(mine, (1, 2, 0, 3)).reshape(1, own_rows, 2, NV)
    return elemental, correlator[:, None, :]


def solution(mesh):
    grid = Mesh(mesh.devices.reshape(8, 2, 4, 4, 2), ("zl", "core", "y", "x", "zh"))
    times = ("zl", "core")
    in_specs = (
        P(times, None, SPACE, None, None, None),
        P(times, None, None, SPACE, None, None, None),
        P(times, SPACE, None, None, None),
        P(times),
        P(),
        P(),
    )
    out_specs = (P(times, SPACE, None, None), P(None, times, None))

    return jax.shard_map(per_device, mesh=grid, in_specs=in_specs, out_specs=out_specs, check_vma=False)
```

```python
import math

import jax
import jax.numpy as jnp
from jax import lax
from jax.experimental import pallas as pl
from jax.experimental.pallas import tpu as pltpu
from jax.sharding import Mesh, PartitionSpec as P


NV = 256
NS = 4
SX = 16
SY = 8
SITES = SX * SY
HALF = NV // 2
VROWS = 6 * HALF
LROWS = 64
KAPPA = 0.05

SPACE = ("y", "x", "zh")
XY = ("y", "x")
CHUNK = 16


def whole():
    return pl.BlockSpec(memory_space=pltpu.VMEM)


def scalar():
    return pl.BlockSpec(memory_space=pltpu.SMEM)


def roll_lanes(value, shift):
    return pltpu.roll(value, shift % SITES, value.ndim - 1)


def ahead_x(value, last):
    return jnp.where(last, roll_lanes(value, SX - 1), roll_lanes(value, -1))


def behind_x(value, first):
    return jnp.where(first, roll_lanes(value, 1 - SX), roll_lanes(value, 1))


def smear_kernel(pick_ref, level_ref, phase_ref, *refs):
    planes, (left_ref, right_ref, link_ref, field_ref, one_ref, two_ref) = refs[:7], refs[7:]
    for index, source in enumerate(planes):
        field_ref[index] = source[pl.ds(0, VROWS), :].astype(jnp.float32)
        link_ref[index, pl.ds(0, LROWS), :] = source[pl.ds(VROWS, LROWS), :].astype(jnp.float32)

    @pl.when(level_ref[0] != 0)
    def _():
        for plane in range(6):
            for part in range(2):
                for row in range(3):
                    for column in range(3):
                        line = link_ref[plane + 1, pl.ds(36 + part * 9 + column * 3 + row, 1), :]
                        at = pl.ds(36 + part * 9 + row * 3 + column, 1)
                        link_ref[plane, at, :] = -line if part else line

    site = lax.broadcasted_iota(jnp.int32, (18, SITES), 1) % SX
    for plane in range(1, 6):
        link_ref[plane, pl.ds(64, 18), :] = behind_x(link_ref[plane, pl.ds(0, 18), :], site == 0)
        link_ref[plane, pl.ds(88, 18), :] = roll_lanes(link_ref[plane, pl.ds(18, 18), :], SX)

    def link(plane, base):
        def get(part, row, column):
            line = link_ref[plane, pl.ds(base + part * 9 + row * 3 + column, 1), :]
            return jnp.broadcast_to(line, (CHUNK, SITES))

        return get

    def packed(matrix):
        return lambda *at: matrix(*at).astype(jnp.bfloat16)

    def apply(total, matrix, field, adjoint):
        for row in range(3):
            for column in range(3):
                if adjoint:
                    real, imag = matrix(0, column, row), matrix(1, column, row)
                    total[0][row] += real * field[0][column] + imag * field[1][column]
                    total[1][row] += real * field[1][column] - imag * field[0][column]
                else:
                    real, imag = matrix(0, row, column), matrix(1, row, column)
                    total[0][row] += real * field[0][column] - imag * field[1][column]
                    total[1][row] += real * field[1][column] + imag * field[0][column]

    column_of = lax.broadcasted_iota(jnp.int32, (CHUNK, SITES), 1) % SX
    last, first = column_of == SX - 1, column_of == 0
    pick = pick_ref[0]

    def each(field, change):
        return [[change(field[part][colour]) for colour in range(3)] for part in range(2)]

    def zeros(kind):
        zero = jnp.zeros((CHUNK, SITES), kind)
        return [[zero for _ in range(3)] for _ in range(2)]

    def narrow(field):
        return each(field, lambda v: v.astype(jnp.bfloat16))

    def sweep(plane, here, above, below):
        total = zeros(jnp.bfloat16)
        middle = narrow(here)
        apply(total, packed(link(plane, 0)), each(middle, lambda v: ahead_x(v, last)), False)
        apply(total, packed(link(plane, 64)), each(middle, lambda v: behind_x(v, first)), True)
        apply(total, packed(link(plane, 18)), each(middle, lambda v: roll_lanes(v, -SX)), False)
        apply(total, packed(link(plane, 88)), each(middle, lambda v: roll_lanes(v, SX)), True)
        apply(total, packed(link(plane, 36)), narrow(above), False)
        apply(total, packed(link(plane - 1, 36)), narrow(below), True)

        def joined(part, colour):
            return (1.0 - 6.0 * KAPPA) * here[part][colour] + KAPPA * total[part][colour].astype(jnp.float32)

        return [[joined(part, colour) for colour in range(3)] for part in range(2)]

    def step(chunk, carry):
        start = pl.multiple_of(chunk * CHUNK, CHUNK)

        def start_field(plane):
            return [
                [field_ref[plane, pl.ds((part * 3 + colour) * HALF + start, CHUNK), :] for colour in range(3)]
                for part in range(2)
            ]

        def stored(ref, plane):
            return [[ref[plane, part * 3 + colour] for colour in range(3)] for part in range(2)]

        for plane in range(1, 6):
            result = sweep(plane, start_field(plane), start_field(plane + 1), start_field(plane - 1))
            for part in range(2):
                for colour in range(3):
                    one_ref[plane, part * 3 + colour] = result[part][colour]
        for plane in range(2, 5):
            result = sweep(plane, stored(one_ref, plane), stored(one_ref, plane + 1), stored(one_ref, plane - 1))
            for part in range(2):
                for colour in range(3):
                    two_ref[plane, part * 3 + colour] = result[part][colour]
        for side in range(2):
            plane = side + 2
            here, above = stored(two_ref, plane), stored(two_ref, plane + 1)
            incoming = [
                [
                    jnp.where(
                        pick == 0,
                        ahead_x(here[part][colour], last),
                        jnp.where(pick == 1, roll_lanes(here[part][colour], -SX), above[part][colour]),
                    )
                    for colour in range(3)
                ]
                for part in range(2)
            ]
            moved = zeros(jnp.float32)
            apply(moved, link(plane, pick * 18), incoming, False)

            def row_of(index):
                return phase_ref[pl.ds(side * 4 + index, 1), :]

            for colour in range(3):

                def put(kind, part, left, real, imag):
                    index = ((kind * 2 + part) * 2 + side) * 3 + colour
                    lanes = pl.ds((index % 2) * SITES, SITES)
                    left_ref[index // 2, pl.ds(start, CHUNK), lanes] = left.astype(jnp.bfloat16)
                    right_ref[index // 2, pl.ds(start, CHUNK), lanes] = real.astype(jnp.bfloat16)
                    right_ref[index // 2, pl.ds(HALF + start, CHUNK), lanes] = imag.astype(jnp.bfloat16)

                def turned(field, base):
                    cosine, sine = row_of(base), row_of(base + 1)
                    return (
                        cosine * field[0][colour] - sine * field[1][colour],
                        cosine * field[1][colour] + sine * field[0][colour],
                    )

                real, imag = turned(moved, 0)
                put(0, 0, here[0][colour], real, imag)
                put(0, 1, here[1][colour], imag, -real)
                real, imag = turned(here, 2)
                put(1, 0, moved[0][colour], real, imag)
                put(1, 1, moved[1][colour], imag, -real)
        return carry

    lax.fori_loop(0, HALF // CHUNK, step, 0)


def room(megabytes):
    return pltpu.CompilerParams(vmem_limit_bytes=megabytes * 2**20)


def smear(pick, level, phase, *planes):
    return pl.pallas_call(
        smear_kernel,
        out_shape=(
            jax.ShapeDtypeStruct((12, HALF, 2 * SITES), jnp.bfloat16),
            jax.ShapeDtypeStruct((12, 2 * HALF, 2 * SITES), jnp.bfloat16),
        ),
        in_specs=[scalar(), scalar()] + [whole()] * (1 + len(planes)),
        out_specs=(whole(), whole()),
        scratch_shapes=[
            pltpu.VMEM((7, 112, SITES), jnp.float32),
            pltpu.VMEM((7, VROWS, SITES), jnp.float32),
            pltpu.VMEM((6, 6, CHUNK, SITES), jnp.float32),
            pltpu.VMEM((5, 6, CHUNK, SITES), jnp.float32),
        ],
        compiler_params=room(14),
        name="smear",
    )(pick, level, phase, *planes)


def pair_kernel(core_ref, own_ref, other_ref, right_ref, out_ref):
    core = core_ref[0]

    def product(ref):
        total = jnp.zeros((HALF, 2 * HALF), jnp.float32)
        for index in range(12):
            total += lax.dot_general(
                ref[index], right_ref[index], (((1,), (1,)), ((), ())), preferred_element_type=jnp.float32
            )
        return total.astype(jnp.bfloat16)

    out_ref[pl.ds(pl.multiple_of(core * HALF, HALF), HALF), :] = product(own_ref)
    out_ref[pl.ds(pl.multiple_of((1 - core) * HALF, HALF), HALF), :] = product(other_ref)


def pair(core, own, other, right):
    return pl.pallas_call(
        pair_kernel,
        out_shape=jax.ShapeDtypeStruct((NV, 2 * HALF), jnp.bfloat16),
        in_specs=[scalar(), whole(), whole(), whole()],
        out_specs=whole(),
        compiler_params=room(8),
        name="pair",
    )(core, own, other, right)


def spread_kernel(level_ref, source_ref, gathered_ref, out_ref):
    slots = source_ref.shape[0]
    for core in range(2):
        own = gathered_ref[level_ref[0] * 2 + core]
        for slot in range(slots):
            out_ref[core * slots + slot, 0] = own
            out_ref[core * slots + slot, 1] = gathered_ref[source_ref[slot]]


def spread(level, source_list, gathered):
    rows = gathered.shape[1]
    return pl.pallas_call(
        spread_kernel,
        out_shape=jax.ShapeDtypeStruct((2 * source_list.shape[0], 2, rows, 2 * HALF), jnp.bfloat16),
        in_specs=[scalar(), scalar(), whole()],
        out_specs=whole(),
        compiler_params=room(4),
        name="spread",
    )(level, source_list, gathered)


def trace_kernel(arrived_ref, block_ref, out_ref, left_ref, source_ref):
    shares, rows = arrived_ref.shape[0] // 2, arrived_ref.shape[2]
    for share in range(shares):
        at = pl.ds(share * rows, rows)
        below = pl.ds(NV + share * rows, rows)
        for half in range(2):
            for part in range(2):
                lanes = pl.ds(part * NV + half * HALF, HALF)
                source_ref[at, lanes] = arrived_ref[half * shares + share, 1, :, pl.ds(part * HALF, HALF)]
            real = arrived_ref[half * shares + share, 0, :, pl.ds(0, HALF)]
            imag = arrived_ref[half * shares + share, 0, :, pl.ds(HALF, HALF)]
            here, there = pl.ds(half * HALF, HALF), pl.ds(NV + half * HALF, HALF)
            left_ref[at, here] = real
            left_ref[at, there] = -imag
            left_ref[below, here] = imag
            left_ref[below, there] = real

    def folded(value):
        return jnp.sum(value.reshape(NV // 8, 8, NV), axis=0)

    totals = [jnp.zeros((8, NV), jnp.float32)] * 2
    for index in range(block_ref.shape[0]):
        block = block_ref[index]
        first = jnp.dot(left_ref[...], block, preferred_element_type=jnp.float32).astype(jnp.bfloat16)
        second = jnp.dot(first, source_ref[...], preferred_element_type=jnp.float32)
        second_real = second[:NV, :NV] - second[NV:, NV:]
        second_imag = second[:NV, NV:] + second[NV:, :NV]
        block_real = block[:NV].astype(jnp.float32)
        block_imag = block[NV:].astype(jnp.float32)
        totals = [
            totals[0] + folded(second_real * block_real + second_imag * block_imag),
            totals[1] + folded(second_imag * block_real - second_real * block_imag),
        ]
    lane = lax.broadcasted_iota(jnp.int32, out_ref.shape, 1)
    out_ref[...] = jnp.where(lane == 0, jnp.sum(totals[0]), jnp.sum(totals[1]))


def trace(arrived, blocks, copies):
    return pl.pallas_call(
        trace_kernel,
        out_shape=jax.ShapeDtypeStruct((copies, 128), jnp.float32),
        in_specs=[whole(), whole()],
        out_specs=whole(),
        scratch_shapes=[pltpu.VMEM((2 * NV, 2 * NV), jnp.bfloat16), pltpu.VMEM((NV, 2 * NV), jnp.bfloat16)],
        compiler_params=room(12),
        name="trace",
    )(arrived, blocks)


def phases(momentum, pick, pair_index, level, extent):
    site = jnp.arange(SITES)
    column = (site % SX).astype(jnp.float32)
    row = (site // SX).astype(jnp.float32)
    moment = momentum.astype(jnp.float32)
    height = (pair_index * 2 + jnp.stack([level, 1 - level])).astype(jnp.float32)
    angle = (
        2.0
        * math.pi
        * (moment[0] * column[None] / SX + moment[1] * row[None] / SY + moment[2] * height[:, None] / extent)
    )
    step = jnp.where(pick == 0, moment[0] / SX, jnp.where(pick == 1, moment[1] / SY, moment[2] / extent))
    sign = jnp.where((level != 0) & (pick == 2), -1.0, 1.0)
    shifted = angle + sign * (2.0 * math.pi) * step
    turns = [jnp.cos(angle), -jnp.sin(angle), -jnp.cos(shifted), jnp.sin(shifted)]
    return (sign * jnp.stack(turns, axis=1)).reshape(8, SITES)


def per_device(vectors, gauge_links, perambulator, directions, momentum, source_list):
    core = lax.axis_index("core")
    level = lax.axis_index("zh")
    pair_index = lax.axis_index(XY)
    pairs = lax.axis_size(XY)
    rows = NV // pairs

    links = gauge_links[0, :, :, 0].reshape(54, SITES).astype(jnp.bfloat16)
    pick_row = jnp.broadcast_to(directions[0].astype(jnp.bfloat16), (LROWS - 54, SITES))
    tail = jnp.concatenate([links, pick_row], axis=0)
    planes_here = vectors[0, :, 0].reshape(6, NV, SITES)
    sites = ("core", "zh")
    same = core == level

    def half_of(index):
        half = lax.dynamic_slice_in_dim(planes_here, index * HALF, HALF, 1).reshape(VROWS, SITES)
        return jnp.concatenate([half, tail], axis=0)

    first_half, second_half = lax.optimization_barrier((half_of(core), half_of(1 - core)))
    cross_sibling = lax.ppermute(second_half, sites, [(1, 2), (2, 1)])
    cross_same = lax.ppermute(first_half, sites, [(1, 0), (2, 3)])

    def moved(plane, distance):
        route = [
            (i * 2 + z, (i + (distance if z == 0 else -distance)) % pairs * 2 + z) for i in range(pairs) for z in (0, 1)
        ]
        return lax.ppermute(plane, SPACE, route)

    taken = lax.ppermute(second_half, sites, [(0, 2), (3, 1)])
    own = jnp.where(same, first_half, taken)
    row_own = (moved(own, 1), own, moved(own, -1), moved(own, -2))
    other = jnp.where(same, cross_same, cross_sibling)
    row_other = (moved(other, 1), other, moved(other, -1))
    planes = [row_own[0], row_other[0], row_own[1], row_other[1], row_own[2], row_other[2], row_own[3]]
    pick = row_own[1][VROWS + 54, 0].astype(jnp.int32)
    phase = phases(momentum, pick, pair_index, level, 2 * pairs)
    left, right = smear(pick[None], level[None], phase, *planes)
    sibling = lax.ppermute(left, "core", [(0, 1), (1, 0)])
    partial_value = pair(core[None], left, sibling, right)

    parts = lax.all_to_all(partial_value, XY, 0, 0, tiled=True).reshape(pairs, rows, 2 * HALF)
    scale = 1.0 / math.sqrt(3 * SITES * 2 * pairs)
    share = (jnp.sum(parts.astype(jnp.float32), axis=0) * scale).astype(jnp.bfloat16)

    slices = lax.axis_size(("zl", "zh"))
    copies = jnp.broadcast_to(share[None], (slices, rows, 2 * HALF))
    gathered = lax.all_to_all(copies, ("zl", "zh"), 0, 0, tiled=True)
    sent = spread(lax.axis_index("zl")[None], source_list, gathered)
    arrived = lax.all_to_all(sent, ("core", "y", "x"), 0, 0, tiled=True)

    space_count = lax.axis_size(SPACE)
    blocks = perambulator[0].reshape(-1, 2 * NV, NV)
    value = trace(arrived, blocks, space_count)
    values = lax.all_to_all(value, SPACE, 0, 0, tiled=True)[:, :2].reshape(pairs, 2, 2)
    per_slot = jnp.sum(values, axis=1) / (NS * NV)
    one_hot = (source_list[:, None] == jnp.arange(source_list.shape[0])[None]).astype(jnp.float32)
    correlator = jnp.sum(per_slot[:, :, None] * one_hot[:, None, :], axis=0)

    own_rows = NV // space_count
    mine = lax.dynamic_index_in_dim(arrived.reshape(2, pairs, 2, rows, 2, HALF)[:, :, 0], pair_index, 1, keepdims=False)
    mine = lax.dynamic_slice_in_dim(mine, level * own_rows, own_rows, 1)
    elemental = jnp.transpose(mine, (1, 2, 0, 3)).reshape(1, own_rows, 2, NV)
    return elemental, correlator[:, None, :]


def solution(mesh):
    grid = Mesh(mesh.devices.reshape(8, 2, 4, 4, 2), ("zl", "core", "y", "x", "zh"))
    times = ("zl", "core")
    in_specs = (
        P(times, None, SPACE, None, None, None),
        P(times, None, None, SPACE, None, None, None),
        P(times, SPACE, None, None, None),
        P(times),
        P(),
        P(),
    )
    out_specs = (P(times, SPACE, None, None), P(None, times, None))

    return jax.shard_map(per_device, mesh=grid, in_specs=in_specs, out_specs=out_specs, check_vma=False)
```

```python
import functools
import math

import jax
import jax.numpy as jnp
from jax import lax
from jax.experimental import pallas as pl
from jax.experimental.pallas import tpu as pltpu
from jax.sharding import Mesh, PartitionSpec as P


NV = 256
NS = 4
SX = 16
SY = 8
SITES = SX * SY
HALF = NV // 2
VROWS = 6 * HALF
LROWS = 64
KAPPA = 0.05

SPACE = ("y", "x", "zh")
XY = ("y", "x")
CHUNK = 16
PARTS = 2
PART = HALF // PARTS
PROWS = 6 * PART


def whole():
    return pl.BlockSpec(memory_space=pltpu.VMEM)


def scalar():
    return pl.BlockSpec(memory_space=pltpu.SMEM)


def roll_lanes(value, shift):
    return pltpu.roll(value, shift % SITES, value.ndim - 1)


def ahead_x(value, last):
    return jnp.where(last, roll_lanes(value, SX - 1), roll_lanes(value, -1))


def behind_x(value, first):
    return jnp.where(first, roll_lanes(value, 1 - SX), roll_lanes(value, 1))


def smear_kernel(turn, pick_ref, level_ref, phase_ref, *refs):
    own, other, tails = refs[0:4], refs[4:7], refs[7:10]
    left_ref, right_ref, link_ref, field_ref, one_ref, two_ref = refs[10:]
    for index in range(7):
        if index % 2:
            field_ref[index] = other[index // 2][pl.ds(0, PROWS), :].astype(jnp.float32)
            links = tails[index // 2][pl.ds(PROWS, LROWS), :]
        else:
            source = own[index // 2]
            for field in range(6):
                rows = source[pl.ds(field * HALF + turn * PART, PART), :]
                field_ref[index, pl.ds(field * PART, PART), :] = rows.astype(jnp.float32)
            links = source[pl.ds(VROWS, LROWS), :]
        link_ref[index, pl.ds(0, LROWS), :] = links.astype(jnp.float32)

    @pl.when(level_ref[0] != 0)
    def _():
        for plane in range(6):
            for part in range(2):
                for row in range(3):
                    for column in range(3):
                        line = link_ref[plane + 1, pl.ds(36 + part * 9 + column * 3 + row, 1), :]
                        at = pl.ds(36 + part * 9 + row * 3 + column, 1)
                        link_ref[plane, at, :] = -line if part else line

    site = lax.broadcasted_iota(jnp.int32, (18, SITES), 1) % SX
    for plane in range(1, 6):
        link_ref[plane, pl.ds(64, 18), :] = behind_x(link_ref[plane, pl.ds(0, 18), :], site == 0)
        link_ref[plane, pl.ds(88, 18), :] = roll_lanes(link_ref[plane, pl.ds(18, 18), :], SX)

    def link(plane, base):
        def get(part, row, column):
            line = link_ref[plane, pl.ds(base + part * 9 + row * 3 + column, 1), :]
            return jnp.broadcast_to(line, (CHUNK, SITES))

        return get

    def packed(matrix):
        return lambda *at: matrix(*at).astype(jnp.bfloat16)

    def apply(total, matrix, field, adjoint):
        for row in range(3):
            for column in range(3):
                if adjoint:
                    real, imag = matrix(0, column, row), matrix(1, column, row)
                    total[0][row] += real * field[0][column] + imag * field[1][column]
                    total[1][row] += real * field[1][column] - imag * field[0][column]
                else:
                    real, imag = matrix(0, row, column), matrix(1, row, column)
                    total[0][row] += real * field[0][column] - imag * field[1][column]
                    total[1][row] += real * field[1][column] + imag * field[0][column]

    column_of = lax.broadcasted_iota(jnp.int32, (CHUNK, SITES), 1) % SX
    last, first = column_of == SX - 1, column_of == 0
    pick = pick_ref[0]

    def each(field, change):
        return [[change(field[part][colour]) for colour in range(3)] for part in range(2)]

    def zeros(kind):
        zero = jnp.zeros((CHUNK, SITES), kind)
        return [[zero for _ in range(3)] for _ in range(2)]

    def narrow(field):
        return each(field, lambda v: v.astype(jnp.bfloat16))

    def sweep(plane, here, above, below):
        total = zeros(jnp.bfloat16)
        middle = narrow(here)
        apply(total, packed(link(plane, 0)), each(middle, lambda v: ahead_x(v, last)), False)
        apply(total, packed(link(plane, 64)), each(middle, lambda v: behind_x(v, first)), True)
        apply(total, packed(link(plane, 18)), each(middle, lambda v: roll_lanes(v, -SX)), False)
        apply(total, packed(link(plane, 88)), each(middle, lambda v: roll_lanes(v, SX)), True)
        apply(total, packed(link(plane, 36)), narrow(above), False)
        apply(total, packed(link(plane - 1, 36)), narrow(below), True)

        def joined(part, colour):
            return (1.0 - 6.0 * KAPPA) * here[part][colour] + KAPPA * total[part][colour].astype(jnp.float32)

        return [[joined(part, colour) for colour in range(3)] for part in range(2)]

    def step(chunk, carry):
        start = pl.multiple_of(chunk * CHUNK, CHUNK)

        def start_field(plane):
            return [
                [field_ref[plane, pl.ds((part * 3 + colour) * PART + start, CHUNK), :] for colour in range(3)]
                for part in range(2)
            ]

        def stored(ref, plane):
            return [[ref[plane, part * 3 + colour] for colour in range(3)] for part in range(2)]

        for plane in range(1, 6):
            result = sweep(plane, start_field(plane), start_field(plane + 1), start_field(plane - 1))
            for part in range(2):
                for colour in range(3):
                    one_ref[plane, part * 3 + colour] = result[part][colour]
        for plane in range(2, 5):
            result = sweep(plane, stored(one_ref, plane), stored(one_ref, plane + 1), stored(one_ref, plane - 1))
            for part in range(2):
                for colour in range(3):
                    two_ref[plane, part * 3 + colour] = result[part][colour]
        for side in range(2):
            plane = side + 2
            here, above = stored(two_ref, plane), stored(two_ref, plane + 1)
            incoming = [
                [
                    jnp.where(
                        pick == 0,
                        ahead_x(here[part][colour], last),
                        jnp.where(pick == 1, roll_lanes(here[part][colour], -SX), above[part][colour]),
                    )
                    for colour in range(3)
                ]
                for part in range(2)
            ]
            moved = zeros(jnp.float32)
            apply(moved, link(plane, pick * 18), incoming, False)

            def row_of(index):
                return phase_ref[pl.ds(side * 4 + index, 1), :]

            for colour in range(3):

                def put(kind, part, left, real, imag):
                    index = ((kind * 2 + part) * 2 + side) * 3 + colour
                    lanes = pl.ds((index % 2) * SITES, SITES)
                    left_ref[index // 2, pl.ds(start, CHUNK), lanes] = left.astype(jnp.bfloat16)
                    right_ref[index // 2, pl.ds(start, CHUNK), lanes] = real.astype(jnp.bfloat16)
                    right_ref[index // 2, pl.ds(PART + start, CHUNK), lanes] = imag.astype(jnp.bfloat16)

                def turned(field, base):
                    cosine, sine = row_of(base), row_of(base + 1)
                    return (
                        cosine * field[0][colour] - sine * field[1][colour],
                        cosine * field[1][colour] + sine * field[0][colour],
                    )

                real, imag = turned(moved, 0)
                put(0, 0, here[0][colour], real, imag)
                put(0, 1, here[1][colour], imag, -real)
                real, imag = turned(here, 2)
                put(1, 0, moved[0][colour], real, imag)
                put(1, 1, moved[1][colour], imag, -real)
        return carry

    lax.fori_loop(0, PART // CHUNK, step, 0)


def room(megabytes):
    return pltpu.CompilerParams(vmem_limit_bytes=megabytes * 2**20)


def smear(turn, pick, level, phase, own, other, tails):
    planes = (*own, *other, *tails)
    return pl.pallas_call(
        functools.partial(smear_kernel, turn),
        out_shape=(
            jax.ShapeDtypeStruct((12, PART, 2 * SITES), jnp.bfloat16),
            jax.ShapeDtypeStruct((12, 2 * PART, 2 * SITES), jnp.bfloat16),
        ),
        in_specs=[scalar(), scalar()] + [whole()] * (1 + len(planes)),
        out_specs=(whole(), whole()),
        scratch_shapes=[
            pltpu.VMEM((7, 112, SITES), jnp.float32),
            pltpu.VMEM((7, PROWS, SITES), jnp.float32),
            pltpu.VMEM((6, 6, CHUNK, SITES), jnp.float32),
            pltpu.VMEM((5, 6, CHUNK, SITES), jnp.float32),
        ],
        compiler_params=room(12),
        cost_estimate=pl.CostEstimate(flops=10**7, bytes_accessed=10**7, transcendentals=0),
        name="smear",
    )(pick, level, phase, *planes)


def pair_kernel(core_ref, *refs):
    core, out_ref = core_ref[0], refs[-1]
    own, other, right = refs[0:2], refs[2:4], refs[4:6]

    def product(left):
        total = jnp.zeros((HALF, 2 * HALF), jnp.float32)
        for index in range(12):
            rows = jnp.concatenate([ref[index] for ref in left], axis=0)
            columns = jnp.concatenate(
                [ref[index, pl.ds(part * PART, PART), :] for part in range(2) for ref in right], axis=0
            )
            total += lax.dot_general(rows, columns, (((1,), (1,)), ((), ())), preferred_element_type=jnp.float32)
        return total.astype(jnp.bfloat16)

    out_ref[pl.ds(pl.multiple_of(core * HALF, HALF), HALF), :] = product(own)
    out_ref[pl.ds(pl.multiple_of((1 - core) * HALF, HALF), HALF), :] = product(other)


def pair(core, own, other, right):
    return pl.pallas_call(
        pair_kernel,
        out_shape=jax.ShapeDtypeStruct((NV, 2 * HALF), jnp.bfloat16),
        in_specs=[scalar()] + [whole()] * 6,
        out_specs=whole(),
        compiler_params=room(8),
        name="pair",
    )(core, *own, *other, *right)


def spread_kernel(level_ref, source_ref, gathered_ref, out_ref):
    slots = source_ref.shape[0]
    for core in range(2):
        own = gathered_ref[level_ref[0] * 2 + core]
        for slot in range(slots):
            out_ref[core * slots + slot, 0] = own
            out_ref[core * slots + slot, 1] = gathered_ref[source_ref[slot]]


def spread(level, source_list, gathered):
    rows = gathered.shape[1]
    return pl.pallas_call(
        spread_kernel,
        out_shape=jax.ShapeDtypeStruct((2 * source_list.shape[0], 2, rows, 2 * HALF), jnp.bfloat16),
        in_specs=[scalar(), scalar(), whole()],
        out_specs=whole(),
        compiler_params=room(4),
        name="spread",
    )(level, source_list, gathered)


def trace_kernel(arrived_ref, block_ref, out_ref, left_ref, source_ref):
    shares, rows = arrived_ref.shape[0] // 2, arrived_ref.shape[2]
    for share in range(shares):
        at = pl.ds(share * rows, rows)
        below = pl.ds(NV + share * rows, rows)
        for half in range(2):
            for part in range(2):
                lanes = pl.ds(part * NV + half * HALF, HALF)
                source_ref[at, lanes] = arrived_ref[half * shares + share, 1, :, pl.ds(part * HALF, HALF)]
            real = arrived_ref[half * shares + share, 0, :, pl.ds(0, HALF)]
            imag = arrived_ref[half * shares + share, 0, :, pl.ds(HALF, HALF)]
            here, there = pl.ds(half * HALF, HALF), pl.ds(NV + half * HALF, HALF)
            left_ref[at, here] = real
            left_ref[at, there] = -imag
            left_ref[below, here] = imag
            left_ref[below, there] = real

    def folded(value):
        return jnp.sum(value.reshape(NV // 8, 8, NV), axis=0)

    totals = [jnp.zeros((8, NV), jnp.float32)] * 2
    for index in range(block_ref.shape[0]):
        block = block_ref[index]
        first = jnp.dot(left_ref[...], block, preferred_element_type=jnp.float32).astype(jnp.bfloat16)
        second = jnp.dot(first, source_ref[...], preferred_element_type=jnp.float32)
        second_real = second[:NV, :NV] - second[NV:, NV:]
        second_imag = second[:NV, NV:] + second[NV:, :NV]
        block_real = block[:NV].astype(jnp.float32)
        block_imag = block[NV:].astype(jnp.float32)
        totals = [
            totals[0] + folded(second_real * block_real + second_imag * block_imag),
            totals[1] + folded(second_imag * block_real - second_real * block_imag),
        ]
    lane = lax.broadcasted_iota(jnp.int32, out_ref.shape, 1)
    out_ref[...] = jnp.where(lane == 0, jnp.sum(totals[0]), jnp.sum(totals[1]))


def trace(arrived, blocks, copies):
    return pl.pallas_call(
        trace_kernel,
        out_shape=jax.ShapeDtypeStruct((copies, 128), jnp.float32),
        in_specs=[whole(), whole()],
        out_specs=whole(),
        scratch_shapes=[pltpu.VMEM((2 * NV, 2 * NV), jnp.bfloat16), pltpu.VMEM((NV, 2 * NV), jnp.bfloat16)],
        compiler_params=room(12),
        name="trace",
    )(arrived, blocks)


def phases(momentum, pick, pair_index, level, extent):
    site = jnp.arange(SITES)
    column = (site % SX).astype(jnp.float32)
    row = (site // SX).astype(jnp.float32)
    moment = momentum.astype(jnp.float32)
    height = (pair_index * 2 + jnp.stack([level, 1 - level])).astype(jnp.float32)
    angle = (
        2.0
        * math.pi
        * (moment[0] * column[None] / SX + moment[1] * row[None] / SY + moment[2] * height[:, None] / extent)
    )
    step = jnp.where(pick == 0, moment[0] / SX, jnp.where(pick == 1, moment[1] / SY, moment[2] / extent))
    sign = jnp.where((level != 0) & (pick == 2), -1.0, 1.0)
    shifted = angle + sign * (2.0 * math.pi) * step
    turns = [jnp.cos(angle), -jnp.sin(angle), -jnp.cos(shifted), jnp.sin(shifted)]
    return (sign * jnp.stack(turns, axis=1)).reshape(8, SITES)


def per_device(vectors, gauge_links, perambulator, directions, momentum, source_list):
    core = lax.axis_index("core")
    level = lax.axis_index("zh")
    pair_index = lax.axis_index(XY)
    pairs = lax.axis_size(XY)
    rows = NV // pairs

    links = gauge_links[0, :, :, 0].reshape(54, SITES).astype(jnp.bfloat16)
    pick_row = jnp.broadcast_to(directions[0].astype(jnp.bfloat16), (LROWS - 54, SITES))
    tail = jnp.concatenate([links, pick_row], axis=0)
    planes_here = vectors[0, :, 0].reshape(6, NV, SITES)
    sites = ("core", "zh")
    same = core == level

    def half_of(index):
        half = lax.dynamic_slice_in_dim(planes_here, index * HALF, HALF, 1).reshape(VROWS, SITES)
        return jnp.concatenate([half, tail], axis=0)

    def part_of(index, turn):
        rows = lax.dynamic_slice_in_dim(planes_here, index * HALF + turn * PART, PART, 1).reshape(PROWS, SITES)
        return rows if turn else jnp.concatenate([rows, tail], axis=0)

    def moved(plane, distance):
        route = [
            (i * 2 + z, (i + (distance if z == 0 else -distance)) % pairs * 2 + z) for i in range(pairs) for z in (0, 1)
        ]
        return lax.ppermute(plane, SPACE, route)

    sends = [(part_of(1 - core, turn), part_of(core, turn)) for turn in range(PARTS)]
    first_half, second_half, sends = lax.optimization_barrier((half_of(core), half_of(1 - core), sends))
    other = []
    for turn in range(PARTS):
        cross_sibling = lax.ppermute(sends[turn][0], sites, [(1, 2), (2, 1)])
        cross_same = lax.ppermute(sends[turn][1], sites, [(1, 0), (2, 3)])
        other.append((cross_sibling, cross_same))
    taken = lax.ppermute(second_half, sites, [(0, 2), (3, 1)])
    own = jnp.where(same, first_half, taken)
    row_own = (moved(own, 1), own, moved(own, -1), moved(own, -2))
    row_other = []
    for turn in range(PARTS):
        plane = jnp.where(same, other[turn][1], other[turn][0])
        row_other.append((moved(plane, 1), plane, moved(plane, -1)))
    pick = row_own[1][VROWS + 54, 0].astype(jnp.int32)
    phase = phases(momentum, pick, pair_index, level, 2 * pairs)
    left, right, sibling = [], [], []
    for turn in range(PARTS):
        results = smear(turn, pick[None], level[None], phase, row_own, row_other[turn], row_other[0])
        left.append(results[0])
        right.append(results[1])
        sibling.append(lax.ppermute(results[0], "core", [(0, 1), (1, 0)]))
    partial_value = pair(core[None], left, sibling, right)

    parts = lax.all_to_all(partial_value, XY, 0, 0, tiled=True).reshape(pairs, rows, 2 * HALF)
    scale = 1.0 / math.sqrt(3 * SITES * 2 * pairs)
    share = (jnp.sum(parts.astype(jnp.float32), axis=0) * scale).astype(jnp.bfloat16)

    slices = lax.axis_size(("zl", "zh"))
    copies = jnp.broadcast_to(share[None], (slices, rows, 2 * HALF))
    gathered = lax.all_to_all(copies, ("zl", "zh"), 0, 0, tiled=True)
    sent = spread(lax.axis_index("zl")[None], source_list, gathered)
    arrived = lax.all_to_all(sent, ("core", "y", "x"), 0, 0, tiled=True)

    space_count = lax.axis_size(SPACE)
    blocks = perambulator[0].reshape(-1, 2 * NV, NV)
    value = trace(arrived, blocks, space_count)
    values = lax.all_to_all(value, SPACE, 0, 0, tiled=True)[:, :2].reshape(pairs, 2, 2)
    per_slot = jnp.sum(values, axis=1) / (NS * NV)
    one_hot = (source_list[:, None] == jnp.arange(source_list.shape[0])[None]).astype(jnp.float32)
    correlator = jnp.sum(per_slot[:, :, None] * one_hot[:, None, :], axis=0)

    own_rows = NV // space_count
    mine = lax.dynamic_index_in_dim(arrived.reshape(2, pairs, 2, rows, 2, HALF)[:, :, 0], pair_index, 1, keepdims=False)
    mine = lax.dynamic_slice_in_dim(mine, level * own_rows, own_rows, 1)
    elemental = jnp.transpose(mine, (1, 2, 0, 3)).reshape(1, own_rows, 2, NV)
    return elemental, correlator[:, None, :]


def solution(mesh):
    grid = Mesh(mesh.devices.reshape(8, 2, 4, 4, 2), ("zl", "core", "y", "x", "zh"))
    times = ("zl", "core")
    in_specs = (
        P(times, None, SPACE, None, None, None),
        P(times, None, None, SPACE, None, None, None),
        P(times, SPACE, None, None, None),
        P(times),
        P(),
        P(),
    )
    out_specs = (P(times, SPACE, None, None), P(None, times, None))

    return jax.shard_map(per_device, mesh=grid, in_specs=in_specs, out_specs=out_specs, check_vma=False)
```

```python
import math

import jax
import jax.numpy as jnp
from jax import lax
from jax.experimental import pallas as pl
from jax.experimental.pallas import tpu as pltpu
from jax.sharding import Mesh, PartitionSpec as P


NV = 256
NS = 4
SX = 16
SY = 8
SITES = SX * SY
HALF = NV // 2
VROWS = 6 * HALF
LROWS = 64
KAPPA = 0.05

SPACE = ("y", "x", "zh")
XY = ("y", "x")
CHUNK = 32


def whole():
    return pl.BlockSpec(memory_space=pltpu.VMEM)


def scalar():
    return pl.BlockSpec(memory_space=pltpu.SMEM)


def roll_lanes(value, shift):
    return pltpu.roll(value, shift % SITES, value.ndim - 1)


def ahead_x(value, last):
    return jnp.where(last, roll_lanes(value, SX - 1), roll_lanes(value, -1))


def behind_x(value, first):
    return jnp.where(first, roll_lanes(value, 1 - SX), roll_lanes(value, 1))


def smear_kernel(pick_ref, level_ref, phase_ref, *refs):
    planes, (left_ref, right_ref, link_ref, field_ref, one_ref, two_ref) = refs[:7], refs[7:]
    for index, source in enumerate(planes):
        field_ref[index] = source[pl.ds(0, VROWS), :].astype(jnp.float32)
        link_ref[index, pl.ds(0, LROWS), :] = source[pl.ds(VROWS, LROWS), :].astype(jnp.float32)

    @pl.when(level_ref[0] != 0)
    def _():
        for plane in range(6):
            for part in range(2):
                for row in range(3):
                    for column in range(3):
                        line = link_ref[plane + 1, pl.ds(36 + part * 9 + column * 3 + row, 1), :]
                        at = pl.ds(36 + part * 9 + row * 3 + column, 1)
                        link_ref[plane, at, :] = -line if part else line

    site = lax.broadcasted_iota(jnp.int32, (18, SITES), 1) % SX
    for plane in range(1, 6):
        link_ref[plane, pl.ds(64, 18), :] = behind_x(link_ref[plane, pl.ds(0, 18), :], site == 0)
        link_ref[plane, pl.ds(88, 18), :] = roll_lanes(link_ref[plane, pl.ds(18, 18), :], SX)

    def link(plane, base):
        def get(part, row, column):
            line = link_ref[plane, pl.ds(base + part * 9 + row * 3 + column, 1), :]
            return jnp.broadcast_to(line, (CHUNK, SITES))

        return get

    def packed(matrix):
        return lambda *at: matrix(*at).astype(jnp.bfloat16)

    def apply(total, matrix, field, adjoint):
        for row in range(3):
            for column in range(3):
                if adjoint:
                    real, imag = matrix(0, column, row), matrix(1, column, row)
                    total[0][row] += real * field[0][column] + imag * field[1][column]
                    total[1][row] += real * field[1][column] - imag * field[0][column]
                else:
                    real, imag = matrix(0, row, column), matrix(1, row, column)
                    total[0][row] += real * field[0][column] - imag * field[1][column]
                    total[1][row] += real * field[1][column] + imag * field[0][column]

    column_of = lax.broadcasted_iota(jnp.int32, (CHUNK, SITES), 1) % SX
    last, first = column_of == SX - 1, column_of == 0
    pick = pick_ref[0]

    def each(field, change):
        return [[change(field[part][colour]) for colour in range(3)] for part in range(2)]

    def zeros(kind):
        zero = jnp.zeros((CHUNK, SITES), kind)
        return [[zero for _ in range(3)] for _ in range(2)]

    def narrow(field):
        return each(field, lambda v: v.astype(jnp.bfloat16))

    def sweep(plane, here, above, below):
        total = zeros(jnp.bfloat16)
        middle = narrow(here)
        apply(total, packed(link(plane, 0)), each(middle, lambda v: ahead_x(v, last)), False)
        apply(total, packed(link(plane, 64)), each(middle, lambda v: behind_x(v, first)), True)
        apply(total, packed(link(plane, 18)), each(middle, lambda v: roll_lanes(v, -SX)), False)
        apply(total, packed(link(plane, 88)), each(middle, lambda v: roll_lanes(v, SX)), True)
        apply(total, packed(link(plane, 36)), narrow(above), False)
        apply(total, packed(link(plane - 1, 36)), narrow(below), True)

        def joined(part, colour):
            return (1.0 - 6.0 * KAPPA) * here[part][colour] + KAPPA * total[part][colour].astype(jnp.float32)

        return [[joined(part, colour) for colour in range(3)] for part in range(2)]

    def step(chunk, carry):
        start = pl.multiple_of(chunk * CHUNK, CHUNK)

        def start_field(plane):
            return [
                [field_ref[plane, pl.ds((part * 3 + colour) * HALF + start, CHUNK), :] for colour in range(3)]
                for part in range(2)
            ]

        def stored(ref, plane):
            return [[ref[plane, part * 3 + colour] for colour in range(3)] for part in range(2)]

        for plane in range(1, 6):
            result = sweep(plane, start_field(plane), start_field(plane + 1), start_field(plane - 1))
            for part in range(2):
                for colour in range(3):
                    one_ref[plane, part * 3 + colour] = result[part][colour]
        for plane in range(2, 5):
            result = sweep(plane, stored(one_ref, plane), stored(one_ref, plane + 1), stored(one_ref, plane - 1))
            for part in range(2):
                for colour in range(3):
                    two_ref[plane, part * 3 + colour] = result[part][colour]
        for side in range(2):
            plane = side + 2
            here, above = stored(two_ref, plane), stored(two_ref, plane + 1)
            incoming = [
                [
                    jnp.where(
                        pick == 0,
                        ahead_x(here[part][colour], last),
                        jnp.where(pick == 1, roll_lanes(here[part][colour], -SX), above[part][colour]),
                    )
                    for colour in range(3)
                ]
                for part in range(2)
            ]
            moved = zeros(jnp.float32)
            apply(moved, link(plane, pick * 18), incoming, False)

            def row_of(index):
                return phase_ref[pl.ds(side * 4 + index, 1), :]

            for colour in range(3):

                def put(kind, part, left, real, imag):
                    index = ((kind * 2 + part) * 2 + side) * 3 + colour
                    lanes = pl.ds((index % 2) * SITES, SITES)
                    left_ref[index // 2, pl.ds(start, CHUNK), lanes] = left.astype(jnp.bfloat16)
                    right_ref[index // 2, pl.ds(start, CHUNK), lanes] = real.astype(jnp.bfloat16)
                    right_ref[index // 2, pl.ds(HALF + start, CHUNK), lanes] = imag.astype(jnp.bfloat16)

                def turned(field, base):
                    cosine, sine = row_of(base), row_of(base + 1)
                    return (
                        cosine * field[0][colour] - sine * field[1][colour],
                        cosine * field[1][colour] + sine * field[0][colour],
                    )

                real, imag = turned(moved, 0)
                put(0, 0, here[0][colour], real, imag)
                put(0, 1, here[1][colour], imag, -real)
                real, imag = turned(here, 2)
                put(1, 0, moved[0][colour], real, imag)
                put(1, 1, moved[1][colour], imag, -real)
        return carry

    lax.fori_loop(0, HALF // CHUNK, step, 0)


def room(megabytes):
    return pltpu.CompilerParams(vmem_limit_bytes=megabytes * 2**20)


def smear(pick, level, phase, *planes):
    return pl.pallas_call(
        smear_kernel,
        out_shape=(
            jax.ShapeDtypeStruct((12, HALF, 2 * SITES), jnp.bfloat16),
            jax.ShapeDtypeStruct((12, 2 * HALF, 2 * SITES), jnp.bfloat16),
        ),
        in_specs=[scalar(), scalar()] + [whole()] * (1 + len(planes)),
        out_specs=(whole(), whole()),
        scratch_shapes=[
            pltpu.VMEM((7, 112, SITES), jnp.float32),
            pltpu.VMEM((7, VROWS, SITES), jnp.float32),
            pltpu.VMEM((6, 6, CHUNK, SITES), jnp.float32),
            pltpu.VMEM((5, 6, CHUNK, SITES), jnp.float32),
        ],
        compiler_params=room(14),
        name="smear",
    )(pick, level, phase, *planes)


def pair_kernel(core_ref, own_ref, other_ref, right_ref, out_ref):
    core = core_ref[0]

    def product(ref):
        total = jnp.zeros((HALF, 2 * HALF), jnp.float32)
        for index in range(12):
            total += lax.dot_general(
                ref[index], right_ref[index], (((1,), (1,)), ((), ())), preferred_element_type=jnp.float32
            )
        return total.astype(jnp.bfloat16)

    out_ref[pl.ds(pl.multiple_of(core * HALF, HALF), HALF), :] = product(own_ref)
    out_ref[pl.ds(pl.multiple_of((1 - core) * HALF, HALF), HALF), :] = product(other_ref)


def pair(core, own, other, right):
    return pl.pallas_call(
        pair_kernel,
        out_shape=jax.ShapeDtypeStruct((NV, 2 * HALF), jnp.bfloat16),
        in_specs=[scalar(), whole(), whole(), whole()],
        out_specs=whole(),
        compiler_params=room(8),
        name="pair",
    )(core, own, other, right)


def spread_kernel(level_ref, source_ref, gathered_ref, out_ref):
    slots = source_ref.shape[0]
    for core in range(2):
        own = gathered_ref[level_ref[0] * 2 + core]
        for slot in range(slots):
            out_ref[core * slots + slot, 0] = own
            out_ref[core * slots + slot, 1] = gathered_ref[source_ref[slot]]


def spread(level, source_list, gathered):
    rows = gathered.shape[1]
    return pl.pallas_call(
        spread_kernel,
        out_shape=jax.ShapeDtypeStruct((2 * source_list.shape[0], 2, rows, 2 * HALF), jnp.bfloat16),
        in_specs=[scalar(), scalar(), whole()],
        out_specs=whole(),
        compiler_params=room(4),
        name="spread",
    )(level, source_list, gathered)


def trace_kernel(arrived_ref, block_ref, out_ref, left_ref, source_ref):
    shares, rows = arrived_ref.shape[0] // 2, arrived_ref.shape[2]
    for share in range(shares):
        at = pl.ds(share * rows, rows)
        below = pl.ds(NV + share * rows, rows)
        for half in range(2):
            for part in range(2):
                lanes = pl.ds(part * NV + half * HALF, HALF)
                source_ref[at, lanes] = arrived_ref[half * shares + share, 1, :, pl.ds(part * HALF, HALF)]
            real = arrived_ref[half * shares + share, 0, :, pl.ds(0, HALF)]
            imag = arrived_ref[half * shares + share, 0, :, pl.ds(HALF, HALF)]
            here, there = pl.ds(half * HALF, HALF), pl.ds(NV + half * HALF, HALF)
            left_ref[at, here] = real
            left_ref[at, there] = -imag
            left_ref[below, here] = imag
            left_ref[below, there] = real

    def folded(value):
        return jnp.sum(value.reshape(NV // 8, 8, NV), axis=0)

    totals = [jnp.zeros((8, NV), jnp.float32)] * 2
    for index in range(block_ref.shape[0]):
        block = block_ref[index]
        first = jnp.dot(left_ref[...], block, preferred_element_type=jnp.float32).astype(jnp.bfloat16)
        second = jnp.dot(first, source_ref[...], preferred_element_type=jnp.float32)
        second_real = second[:NV, :NV] - second[NV:, NV:]
        second_imag = second[:NV, NV:] + second[NV:, :NV]
        block_real = block[:NV].astype(jnp.float32)
        block_imag = block[NV:].astype(jnp.float32)
        totals = [
            totals[0] + folded(second_real * block_real + second_imag * block_imag),
            totals[1] + folded(second_imag * block_real - second_real * block_imag),
        ]
    lane = lax.broadcasted_iota(jnp.int32, out_ref.shape, 1)
    out_ref[...] = jnp.where(lane == 0, jnp.sum(totals[0]), jnp.sum(totals[1]))


def trace(arrived, blocks, copies):
    return pl.pallas_call(
        trace_kernel,
        out_shape=jax.ShapeDtypeStruct((copies, 128), jnp.float32),
        in_specs=[whole(), whole()],
        out_specs=whole(),
        scratch_shapes=[pltpu.VMEM((2 * NV, 2 * NV), jnp.bfloat16), pltpu.VMEM((NV, 2 * NV), jnp.bfloat16)],
        compiler_params=room(12),
        name="trace",
    )(arrived, blocks)


def phases(momentum, pick, pair_index, level, extent):
    site = jnp.arange(SITES)
    column = (site % SX).astype(jnp.float32)
    row = (site // SX).astype(jnp.float32)
    moment = momentum.astype(jnp.float32)
    height = (pair_index * 2 + jnp.stack([level, 1 - level])).astype(jnp.float32)
    angle = (
        2.0
        * math.pi
        * (moment[0] * column[None] / SX + moment[1] * row[None] / SY + moment[2] * height[:, None] / extent)
    )
    step = jnp.where(pick == 0, moment[0] / SX, jnp.where(pick == 1, moment[1] / SY, moment[2] / extent))
    sign = jnp.where((level != 0) & (pick == 2), -1.0, 1.0)
    shifted = angle + sign * (2.0 * math.pi) * step
    turns = [jnp.cos(angle), -jnp.sin(angle), -jnp.cos(shifted), jnp.sin(shifted)]
    return (sign * jnp.stack(turns, axis=1)).reshape(8, SITES)


def per_device(vectors, gauge_links, perambulator, directions, momentum, source_list):
    core = lax.axis_index("core")
    level = lax.axis_index("zh")
    pair_index = lax.axis_index(XY)
    pairs = lax.axis_size(XY)
    rows = NV // pairs

    links = gauge_links[0, :, :, 0].reshape(54, SITES).astype(jnp.bfloat16)
    pick_row = jnp.broadcast_to(directions[0].astype(jnp.bfloat16), (LROWS - 54, SITES))
    tail = jnp.concatenate([links, pick_row], axis=0)
    planes_here = vectors[0, :, 0].reshape(6, NV, SITES)
    sites = ("core", "zh")
    same = core == level

    def half_of(index):
        half = lax.dynamic_slice_in_dim(planes_here, index * HALF, HALF, 1).reshape(VROWS, SITES)
        return jnp.concatenate([half, tail], axis=0)

    first_half, second_half = lax.optimization_barrier((half_of(core), half_of(1 - core)))
    cross_sibling = lax.ppermute(second_half, sites, [(1, 2), (2, 1)])
    cross_same = lax.ppermute(first_half, sites, [(1, 0), (2, 3)])

    def moved(plane, distance):
        route = [
            (i * 2 + z, (i + (distance if z == 0 else -distance)) % pairs * 2 + z) for i in range(pairs) for z in (0, 1)
        ]
        return lax.ppermute(plane, SPACE, route)

    taken = lax.ppermute(second_half, sites, [(0, 2), (3, 1)])
    own = jnp.where(same, first_half, taken)
    row_own = (moved(own, 1), own, moved(own, -1), moved(own, -2))
    other = jnp.where(same, cross_same, cross_sibling)
    row_other = (moved(other, 1), other, moved(other, -1))
    planes = [row_own[0], row_other[0], row_own[1], row_other[1], row_own[2], row_other[2], row_own[3]]
    pick = row_own[1][VROWS + 54, 0].astype(jnp.int32)
    late_momentum, _ = lax.optimization_barrier((momentum, other))
    phase = phases(late_momentum, pick, pair_index, level, 2 * pairs)
    left, right = smear(pick[None], level[None], phase, *planes)
    sibling = lax.ppermute(left, "core", [(0, 1), (1, 0)])
    partial_value = pair(core[None], left, sibling, right)

    parts = lax.all_to_all(partial_value, XY, 0, 0, tiled=True).reshape(pairs, rows, 2 * HALF)
    scale = 1.0 / math.sqrt(3 * SITES * 2 * pairs)
    share = (jnp.sum(parts.astype(jnp.float32), axis=0) * scale).astype(jnp.bfloat16)

    slices = lax.axis_size(("zl", "zh"))
    copies = jnp.broadcast_to(share[None], (slices, rows, 2 * HALF))
    gathered = lax.all_to_all(copies, ("zl", "zh"), 0, 0, tiled=True)
    sent = spread(lax.axis_index("zl")[None], source_list, gathered)
    arrived = lax.all_to_all(sent, ("core", "y", "x"), 0, 0, tiled=True)

    space_count = lax.axis_size(SPACE)
    blocks = perambulator[0].reshape(-1, 2 * NV, NV)
    value = trace(arrived, blocks, space_count)
    values = lax.all_to_all(value, SPACE, 0, 0, tiled=True)[:, :2].reshape(pairs, 2, 2)
    per_slot = jnp.sum(values, axis=1) / (NS * NV)
    one_hot = (source_list[:, None] == jnp.arange(source_list.shape[0])[None]).astype(jnp.float32)
    correlator = jnp.sum(per_slot[:, :, None] * one_hot[:, None, :], axis=0)

    own_rows = NV // space_count
    mine = lax.dynamic_index_in_dim(arrived.reshape(2, pairs, 2, rows, 2, HALF)[:, :, 0], pair_index, 1, keepdims=False)
    mine = lax.dynamic_slice_in_dim(mine, level * own_rows, own_rows, 1)
    elemental = jnp.transpose(mine, (1, 2, 0, 3)).reshape(1, own_rows, 2, NV)
    return elemental, correlator[:, None, :]


def solution(mesh):
    grid = Mesh(mesh.devices.reshape(8, 2, 4, 4, 2), ("zl", "core", "y", "x", "zh"))
    times = ("zl", "core")
    in_specs = (
        P(times, None, SPACE, None, None, None),
        P(times, None, None, SPACE, None, None, None),
        P(times, SPACE, None, None, None),
        P(times),
        P(),
        P(),
    )
    out_specs = (P(times, SPACE, None, None), P(None, times, None))

    return jax.shard_map(per_device, mesh=grid, in_specs=in_specs, out_specs=out_specs, check_vma=False)
```
